512 devices in a mesh: parts: 512 (over z, y, x, core).
Axes of the slice: x: 4, y: 4, z: 16, core: 2. Of those that a mesh axis runs over, the one named last changes fastest.
Arguments:
- positions: float32 [3, 262144], P(None, 'parts'), may hold values from -6 to 6
- velocity: float32 [3, 262144], P(None, 'parts'), may hold values from -6 to 6
- inv_mass: float32 [262144], P('parts'), may hold values from 0.5 to 4
- swap_lists: int32 [3, 131072], P(None, 'parts'), may hold values from 0 to 511, as said below
- rim_list: int32 [65536], P('parts'), may hold values from 0 to 511, as said below
- contact_pair: int32 [2, 524288], P(None, 'parts'), may hold values from 0 to 767, as said below
- delassus: float32 [4096, 128, 128], P('parts'), as said below
Outputs:
- new_velocity: float32 [3, 262144], P(None, 'parts')
- impulse: float32 [524288], P('parts')
The draws below stay inside these ranges and needn't reach their ends.
Inputs may be any that keep to these rules, and one draw needn't show every extreme that they name: `swap_lists`: the 256 slots of one part at one level are distinct. `rim_list`: the 128 slots of one part are distinct. `contact_pair`: the first index of a contact is a local grain; the two indices differ. `delassus`: tile diagonals lie between 4 and 8.
All inputs are finite; a program needn't handle non-finite values.
Results may differ from the reference program's by a relative error of at most 0.0003.
Values sent between devices are 32-bit elements; how exact they have to be, the bound alone decides.
A program may use at most 64 MiB of HBM per device.

```python
import math
import jax
import jax.numpy as jnp
from jax import lax

GRAIN_DEV = 512
SWAP_ROWS = 256
RIM = 128
TILES_DEV = 8
TILE = 128
CONTACT_DEV = 1024
LEVELS = 3
ITERS = 2
GRAINS = 262144
CONTACTS = 524288


def distinct_slots(key, lists, keep):
    keys = jax.random.split(key, lists)
    return jax.vmap(lambda one: jax.random.permutation(one, GRAIN_DEV)[:keep])(keys).astype(jnp.int32)


def draw_swap_lists(key, part):
    count = GRAINS // GRAIN_DEV
    slots = distinct_slots(jax.random.fold_in(key, 11), LEVELS * count, SWAP_ROWS)
    return slots.reshape(LEVELS, count * SWAP_ROWS)


def draw_rim_list(key, part):
    count = GRAINS // GRAIN_DEV
    return distinct_slots(jax.random.fold_in(key, 23), count, RIM).reshape(count * RIM)


def draw_contact_pair(key, part):
    count = GRAINS // GRAIN_DEV
    key_one, key_two = jax.random.split(jax.random.fold_in(key, 37))
    first = jax.random.randint(key_one, (count, CONTACT_DEV), 0, GRAIN_DEV, dtype=jnp.int32)
    other = jax.random.randint(key_two, (count, CONTACT_DEV), 0, GRAIN_DEV + 2 * RIM - 1, dtype=jnp.int32)
    other = jnp.where(other >= first, other + 1, other)
    return jnp.stack([first, other]).reshape(2, count * CONTACT_DEV)


def draw_delassus(key, part):
    count = GRAINS // GRAIN_DEV
    key_one, key_two = jax.random.split(jax.random.fold_in(key, 41))
    off = 0.15 * jax.random.normal(key_one, (TILES_DEV * count, TILE, TILE), jnp.float32)
    diag = jax.random.uniform(key_two, (TILES_DEV * count, TILE), jnp.float32, 4.0, 8.0)
    eye = jnp.eye(TILE, dtype=jnp.float32)
    return off * (1.0 - eye) + diag[:, :, None] * eye


def steps_of(stream_key, shape, pieces, least, top_value):
    gain, own = 1.0, jax.random.fold_in(stream_key, 6)
    for dim, shards_of in pieces:
        heights = jnp.exp(jax.random.uniform(jax.random.fold_in(own, dim), (shards_of,), jnp.float32, least / len(pieces), top_value / len(pieces)))
        gain = gain * jnp.repeat(heights, shape[dim] // shards_of).reshape([-1 if axis == dim else 1 for axis in range(len(shape))])
    return gain


def centred(own_key, shape, spread, bound, shards=(), kind=jnp.bfloat16):
    entries = spread * jax.random.normal(own_key, shape, jnp.float32)
    if shards:
        entries = entries * steps_of(own_key, shape, shards, -0.22, 0.18)
    return jnp.clip(entries, -bound, bound).astype(kind)


def setup_inputs(seed: int = 0) -> dict:
    key_of = jax.random.split(jax.random.key(seed), 8)
    positions = centred(key_of[0], (3, GRAINS), 1.0, 6.0, ((1, 512),), jnp.float32)
    velocity = centred(key_of[1], (3, GRAINS), 1.0, 6.0, ((1, 512),), jnp.float32)
    inv_mass = jnp.clip(jnp.exp(math.log(4.0) - 2.0794415 * jax.random.uniform(key_of[2], (GRAINS,), jnp.float32) ** steps_of(key_of[2], (GRAINS,), ((0, 512),), -0.2, 0.2)), 0.5, 4.0)
    swap_lists = draw_swap_lists(jax.random.fold_in(key_of[7], 71), 0)
    rim_list = draw_rim_list(jax.random.fold_in(key_of[7], 71), 0)
    contact_pair = draw_contact_pair(jax.random.fold_in(key_of[7], 71), 0)
    delassus = draw_delassus(jax.random.fold_in(key_of[7], 71), 0)
    return {"positions": positions, "velocity": velocity, "inv_mass": inv_mass, "swap_lists": swap_lists, "rim_list": rim_list, "contact_pair": contact_pair, "delassus": delassus}


def shift_down(block):
    zeros = jnp.zeros_like(block[:, :1])
    return jnp.concatenate([zeros, block[:, :-1]], axis=1)


def shift_up(block):
    zeros = jnp.zeros_like(block[:, :1])
    return jnp.concatenate([block[:, 1:], zeros], axis=1)


def extend(field, rows, rim_slots):
    rim_rows = field[:, rows, rim_slots]
    return jnp.concatenate([field, shift_down(rim_rows), shift_up(rim_rows)], axis=2)


def reference(positions, velocity, inv_mass, swap_lists, rim_list, contact_pair, delassus):
    count = GRAINS // GRAIN_DEV
    bits = count.bit_length() - 1
    parts_ids = jnp.arange(count, dtype=jnp.int32)
    rows = parts_ids[:, None]
    pos = positions.reshape(3, count, GRAIN_DEV)
    vel = velocity.reshape(3, count, GRAIN_DEV)
    mass = inv_mass.reshape(1, count, GRAIN_DEV)
    for level in range(LEVELS):
        partner = parts_ids ^ (1 << (bits - 1 - level))
        slots = swap_lists[level].reshape(count, SWAP_ROWS)
        pos = pos.at[:, rows, slots].set(pos[:, rows, slots][:, partner])
        vel = vel.at[:, rows, slots].set(vel[:, rows, slots][:, partner])
        mass = mass.at[:, rows, slots].set(mass[:, rows, slots][:, partner])
    rim_slots = rim_list.reshape(count, RIM)
    ext_pos = extend(pos, rows, rim_slots)
    ext_vel = extend(vel, rows, rim_slots)
    first = contact_pair[0].reshape(count, CONTACT_DEV)
    second = contact_pair[1].reshape(count, CONTACT_DEV)
    normal = ext_pos[:, rows, first] - ext_pos[:, rows, second]
    tiles = delassus.reshape(count, TILES_DEV, TILE, TILE)
    diag = jnp.diagonal(tiles, axis1=2, axis2=3).reshape(count, CONTACT_DEV)
    lam = jnp.zeros((count, CONTACT_DEV), jnp.float32)
    current = vel
    for step in range(ITERS):
        speed = jnp.sum(normal * (ext_vel[:, rows, first] - ext_vel[:, rows, second]), axis=0)
        coupled = jnp.einsum("ptij,ptj->pti", tiles, lam.reshape(count, TILES_DEV, TILE), precision=lax.Precision.HIGHEST).reshape(count, CONTACT_DEV)
        lam = jnp.maximum(0.0, lam - (coupled + speed) / diag)
        force = normal * lam[None]
        partial_value = jnp.zeros((3, count, GRAIN_DEV + 2 * RIM), jnp.float32)
        partial_value = partial_value.at[:, rows, first].add(force).at[:, rows, second].add(-force)
        left_ghost = partial_value[:, :, GRAIN_DEV:GRAIN_DEV + RIM]
        right_ghost = partial_value[:, :, GRAIN_DEV + RIM:]
        incoming = shift_down(right_ghost) + shift_up(left_ghost)
        local = partial_value[:, :, :GRAIN_DEV].at[:, rows, rim_slots].add(incoming)
        current = vel + mass * local
        ext_vel = extend(current, rows, rim_slots)
    return current.reshape(3, GRAINS), lam.reshape(CONTACTS)
```

```python
import jax
import jax.numpy as jnp
from jax import lax
from jax.experimental import pallas as pl
from jax.experimental.pallas import tpu as pltpu
from jax.sharding import PartitionSpec as P

MESH = pl.DeviceIdType.MESH
F32 = jnp.float32
BF16 = jnp.bfloat16
MESSAGES = 15


def split(x):
    head = x.astype(BF16).astype(F32)
    return jnp.concatenate([head, x - head], axis=0).astype(BF16)


def join(y):
    half = y.shape[0] // 2
    return y[:half] + y[half:]


def pick(x, table):
    return join(jnp.dot(split(x), table, preferred_element_type=F32))


def spread(x, table):
    return join(
        lax.dot_general(split(x), table, (((1,), (1,)), ((), ())), preferred_element_type=F32)
    )


def rows8(*pieces):
    have = sum(piece.shape[0] for piece in pieces)
    if have < 8:
        pieces += (jnp.zeros((8 - have, pieces[0].shape[1]), F32),)
    return jnp.concatenate(pieces, axis=0)


def put_one_hot(table, row, base=0):
    extent, width = table.shape
    block = 64

    def step(i, carry):
        slot = lax.broadcasted_iota(jnp.int32, (block, width), 0) + (i * block + base)
        table[pl.ds(pl.multiple_of(i * block, block), block), :] = jnp.where(
            slot == row, 1.0, 0.0
        ).astype(BF16)
        return carry

    lax.fori_loop(0, extent // block, step, 0)


def kernel(
    count,
    pos_hbm, vel_hbm, mass_hbm, lists_hbm, rim_hbm, pair_hbm, tiles_hbm,
    vel_out, lam_out,
    pos_in, vel_in, mass_in, lists_in, rim_in, pair_in, tiles_in,
    ends, swap_tab, peer_tab, rim_tab, rimq_tab, code_tab, tiles_hi, tiles_lo,
    send_a, send_k, send_m, send_b1, send_b2, send_b3, send_c, send_f,
    recv_a, recv_k, recv_m, recv_b1, recv_b2, recv_b3, recv_c, recv_f,
    in_sem, send_sem, recv_sem,
):
    grains = pos_in.shape[1]
    width = rim_in.shape[1]
    contacts = pair_in.shape[1]
    tiles, tile = tiles_in.shape[:2]
    bits = count.bit_length() - 1
    far, mid, near = (1 << (bits - 1 - level) for level in range(3))
    me = lax.axis_index("parts")

    def shifted(base, by):
        return lax.rem(base + (by + count), count)

    def flipped(base, mask):
        return lax.bitwise_xor(base, jnp.int32(mask))

    loads = [
        pltpu.make_async_copy(src, dst, in_sem.at[i])
        for i, (src, dst) in enumerate(
            [
                (lists_hbm, lists_in), (pos_hbm, pos_in), (vel_hbm, vel_in), (mass_hbm, mass_in),
                (rim_hbm, rim_in), (pair_hbm, pair_in), (tiles_hbm, tiles_in),
            ]
        )
    ]
    for load in loads:
        load.start()

    barrier = pltpu.get_barrier_semaphore()
    senders = [
        flipped(me, far), flipped(me, far | mid), flipped(me, mid), flipped(me, near),
        shifted(me, -1), shifted(me, 1),
        flipped(shifted(me, -1), near), flipped(shifted(me, 1), near),
        shifted(me, -2), shifted(me, 2),
    ]
    for sender in senders:
        pl.semaphore_signal(barrier, inc=1, device_id=(sender,), device_id_type=MESH)

    twin = flipped(me, near)
    routes = [
        (send_a, recv_a.at[0], flipped(me, far)),
        (send_a, recv_a.at[1], flipped(me, far | mid)),
        (send_k, recv_k, flipped(me, mid)),
        (send_m, recv_m, twin),
        (send_b1, recv_b1, twin),
        (send_b2, recv_b2.at[0], shifted(me, 1)),
        (send_b2, recv_b2.at[1], shifted(me, -1)),
        (send_b3, recv_b3.at[0], shifted(twin, 1)),
        (send_b3, recv_b3.at[1], shifted(twin, -1)),
        (send_c.at[0], recv_c.at[0], shifted(me, 1)),
        (send_c.at[1], recv_c.at[1], shifted(me, -1)),
        (send_c.at[0], recv_c.at[2], shifted(me, 2)),
        (send_c.at[1], recv_c.at[3], shifted(me, -2)),
        (send_f.at[0], recv_f.at[0], shifted(me, 1)),
        (send_f.at[1], recv_f.at[1], shifted(me, -1)),
    ]
    copies = [
        pltpu.make_async_remote_copy(
            src_ref=src, dst_ref=dst, send_sem=send_sem.at[i], recv_sem=recv_sem.at[i],
            device_id=(target,), device_id_type=MESH,
        )
        for i, (src, dst, target) in enumerate(routes)
    ]

    for load in loads[:5]:
        load.wait()
    swap = [swap_tab.at[level] for level in range(3)]
    for level in range(3):
        put_one_hot(swap[level], lists_in[level : level + 1, :])
    put_one_hot(rim_tab, rim_in[...])
    ones = jnp.ones((8, lists_in.shape[1]), F32)
    keep = [1.0 - spread(ones, swap[level][...])[:1] for level in range(3)]
    state = rows8(pos_in[...], vel_in[...], mass_in[...])
    lists = lists_in[...].astype(F32)
    kept = state * keep[0]
    send_a[...] = pick(state, swap[0][...])
    send_k[...] = jnp.concatenate(
        [kept[:7], jnp.concatenate([lists[0:1], lists[1:2]], axis=1)], axis=0
    )
    order = lax.broadcasted_iota(jnp.int32, (8, lists_in.shape[1]), 1).astype(F32) + 1.0
    rim_code = pick(spread(order, swap[2][...]), rim_tab[...])
    send_m[...] = rim_code
    rim_keep = jnp.where(rim_code[:1] < 0.5, 1.0, 0.0)

    pl.semaphore_wait(barrier, len(senders))
    for i in (0, 1, 2, 3):
        copies[i].start()

    loads[5].wait()
    first, second = pair_in[0:1, :], pair_in[1:2, :]

    def put_ends(i, carry):
        slot = lax.broadcasted_iota(jnp.int32, (32, contacts), 0) + i * 32
        ends[pl.ds(pl.multiple_of(i * 32, 32), 32), :] = (
            jnp.where(slot == first, 1.0, 0.0) - jnp.where(slot == second, 1.0, 0.0)
        ).astype(BF16)
        return carry

    lax.fori_loop(0, ends.shape[0] // 32, put_ends, 0)

    loads[6].wait()
    eye = lax.broadcasted_iota(jnp.int32, (tile, tile), 0) == lax.broadcasted_iota(
        jnp.int32, (tile, tile), 1
    )
    diags = []
    for t in range(tiles):
        block = tiles_in[t]
        head = block.astype(BF16)
        tiles_hi[t * tile : (t + 1) * tile, :] = head
        tiles_lo[t * tile : (t + 1) * tile, :] = (block - head.astype(F32)).astype(BF16)
        diags.append(jnp.sum(jnp.where(eye, block, 0.0), axis=0, keepdims=True))
    diag = jnp.concatenate(diags, axis=1)
    own_tile = lax.broadcasted_iota(jnp.int32, (tiles, contacts), 0) == (
        lax.broadcasted_iota(jnp.int32, (tiles, contacts), 1) // tile
    )

    def coupled(lam):
        table = jnp.concatenate(
            [lam[:, t * tile : (t + 1) * tile] for t in range(tiles)], axis=0
        )
        product = spread(table, tiles_hi[...]) + spread(table, tiles_lo[...])
        return jnp.sum(jnp.where(own_tile, product, 0.0), axis=0, keepdims=True)

    lam = jnp.zeros((1, contacts), F32)
    pull = coupled(lam)

    copies[3].wait_recv()
    put_one_hot(code_tab, recv_m[0:1, :].astype(jnp.int32), 1)
    rimq_tab[...] = jnp.dot(swap[2][...], code_tab[...], preferred_element_type=F32).astype(BF16)

    copies[2].wait_recv()
    peer_lists = recv_k[7:8, :].astype(jnp.int32)
    half = lists_in.shape[1]
    put_one_hot(peer_tab.at[0], peer_lists[:, :half])
    put_one_hot(peer_tab.at[1], peer_lists[:, half:])
    peer_kept = rows8(recv_k[0:7, :])

    copies[1].wait_recv()
    peer = peer_kept + spread(recv_a[1], peer_tab[0])
    crossing = pick(peer, peer_tab[1])
    copies[0].wait_recv()
    state = kept + spread(recv_a[0], swap[0][...])
    state = state * keep[1] + spread(crossing, swap[1][...])

    own_rim = pick(state, rim_tab[...]) * rim_keep
    send_b3[...] = pick(state, rimq_tab[...])
    send_b2[...] = own_rim
    for i in (7, 8, 5, 6):
        copies[i].start()
    send_b1[...] = pick(state, swap[2][...])
    copies[4].start()

    state = state * keep[2]
    copies[4].wait_recv()
    state = state + spread(recv_b1[...], swap[2][...])
    for i in (5, 6, 7, 8):
        copies[i].wait_recv()
    left = jnp.where(me >= 1, recv_b2[0] + recv_b3[0], 0.0)
    right = jnp.where(me <= count - 2, recv_b2[1] + recv_b3[1], 0.0)
    gathered = pick(jnp.concatenate([state, left, right], axis=1), ends[...])
    normal = gathered[0:3]
    relative = gathered[3:6]
    vel, mass = state[3:6], state[6:7]

    speed = jnp.sum(normal * relative, axis=0, keepdims=True)
    lam = jnp.maximum(0.0, lam - (pull + speed) / diag)
    partial = spread(rows8(normal * lam), ends[...])
    local = partial[0:3, :grains]
    ghost_left = partial[0:3, grains : grains + width]
    ghost_right = partial[0:3, grains + width :]
    at_rim = pick(partial[:, :grains], rim_tab[...])[0:3]
    send_c[0] = rows8(ghost_right, at_rim)
    send_c[1] = rows8(ghost_left, at_rim)
    for i in (9, 10, 11, 12):
        copies[i].start()
    pull = coupled(lam)
    for i in (9, 10, 11, 12):
        copies[i].wait_recv()
    zero = jnp.zeros((3, width), F32)
    incoming = jnp.where(me >= 1, recv_c[0, 0:3], zero) + jnp.where(
        me <= count - 2, recv_c[1, 0:3], zero
    )
    current = vel + mass * (local + spread(rows8(incoming), rim_tab[...])[0:3])
    total_left = recv_c[0, 3:6] + ghost_left + jnp.where(me >= 2, recv_c[2, 0:3], zero)
    total_right = recv_c[1, 3:6] + ghost_right + jnp.where(me <= count - 3, recv_c[3, 0:3], zero)
    fresh_left = left[3:6] + left[6:7] * total_left
    fresh_right = right[3:6] + right[6:7] * total_right
    relative = pick(
        rows8(jnp.concatenate([current, fresh_left, fresh_right], axis=1)), ends[...]
    )[0:3]

    speed = jnp.sum(normal * relative, axis=0, keepdims=True)
    lam = jnp.maximum(0.0, lam - (pull + speed) / diag)
    partial = spread(rows8(normal * lam), ends[...])
    send_f[0] = rows8(partial[0:3, grains + width :])
    send_f[1] = rows8(partial[0:3, grains : grains + width])
    for i in (13, 14):
        copies[i].start()
    lam_out[...] = lam
    local = partial[0:3, :grains]
    for i in (13, 14):
        copies[i].wait_recv()
    incoming = jnp.where(me >= 1, recv_f[0, 0:3], zero) + jnp.where(
        me <= count - 2, recv_f[1, 0:3], zero
    )
    vel_out[...] = vel + mass * (local + spread(rows8(incoming), rim_tab[...])[0:3])
    for copy in copies:
        copy.wait_send()


def body(count, positions, velocity, inv_mass, swap_lists, rim_list, contact_pair, delassus):
    grains = positions.shape[1]
    half = swap_lists.shape[1]
    width = rim_list.shape[0]
    contacts = contact_pair.shape[1]
    tiles, tile = delassus.shape[:2]
    args = (
        positions, velocity, inv_mass.reshape(1, grains), swap_lists, rim_list.reshape(1, width),
        contact_pair, delassus,
    )

    def grid(rows, columns):
        return pltpu.VMEM((rows, columns), F32)

    current, lam = pl.pallas_call(
        lambda *refs: kernel(count, *refs),
        out_shape=(
            jax.ShapeDtypeStruct((3, grains), F32),
            jax.ShapeDtypeStruct((1, contacts), F32),
        ),
        in_specs=[pl.BlockSpec(memory_space=pltpu.HBM)] * len(args),
        out_specs=(
            pl.BlockSpec(memory_space=pltpu.VMEM),
            pl.BlockSpec(memory_space=pltpu.VMEM),
        ),
        scratch_shapes=[pltpu.VMEM(arg.shape, arg.dtype) for arg in args]
        + [
            pltpu.VMEM((grains + 2 * width, contacts), BF16),
            pltpu.VMEM((3, grains, half), BF16),
            pltpu.VMEM((2, grains, half), BF16),
            pltpu.VMEM((grains, width), BF16),
            pltpu.VMEM((grains, width), BF16),
            pltpu.VMEM((half, width), BF16),
            pltpu.VMEM((contacts, tile), BF16),
            pltpu.VMEM((contacts, tile), BF16),
            grid(8, half), grid(8, grains), grid(8, width),
            grid(8, half), grid(8, width), grid(8, width),
            pltpu.VMEM((2, 8, width), F32), pltpu.VMEM((2, 8, width), F32),
            pltpu.VMEM((2, 8, half), F32), grid(8, grains), grid(8, width),
            grid(8, half), pltpu.VMEM((2, 8, width), F32), pltpu.VMEM((2, 8, width), F32),
            pltpu.VMEM((4, 8, width), F32), pltpu.VMEM((2, 8, width), F32),
            pltpu.SemaphoreType.DMA((len(args),)),
            pltpu.SemaphoreType.DMA((MESSAGES,)),
            pltpu.SemaphoreType.DMA((MESSAGES,)),
        ],
        compiler_params=pltpu.CompilerParams(
            collective_id=0, has_side_effects=True, vmem_limit_bytes=32 << 20
        ),
        name="contact_step",
    )(*args)
    return current, lam.reshape(contacts)


def solution(mesh):
    count = mesh.shape["parts"]
    in_specs = (
        P(None, "parts"),
        P(None, "parts"),
        P("parts"),
        P(None, "parts"),
        P("parts"),
        P(None, "parts"),
        P("parts", None, None),
    )
    out_specs = (P(None, "parts"), P("parts"))
    return jax.shard_map(
        lambda *args: body(count, *args),
        mesh=mesh, in_specs=in_specs, out_specs=out_specs, check_vma=False,
    )
```

```python
import functools

import jax
import jax.numpy as jnp
from jax import lax
from jax.experimental import pallas as pl
from jax.experimental.pallas import tpu as pltpu
from jax.sharding import PartitionSpec as P

MESH = pl.DeviceIdType.MESH
F32 = jnp.float32
BF16 = jnp.bfloat16
MESSAGES = 18


def split(x):
    head = x.astype(BF16).astype(F32)
    return jnp.concatenate([head, x - head], axis=0).astype(BF16)


def join(y):
    half = y.shape[0] // 2
    return y[:half] + y[half:]


def pick(x, table):
    return join(jnp.dot(split(x), table, preferred_element_type=F32))


def spread(x, table):
    return join(
        lax.dot_general(split(x), table, (((1,), (1,)), ((), ())), preferred_element_type=F32)
    )


def rows8(*pieces):
    have = sum(piece.shape[0] for piece in pieces)
    if have < 8:
        pieces += (jnp.zeros((8 - have, pieces[0].shape[1]), F32),)
    return jnp.concatenate(pieces, axis=0)


def put_one_hot(table, row, base=0):
    extent, width = table.shape
    block = 64

    def step(i, carry):
        slot = lax.broadcasted_iota(jnp.int32, (block, width), 0) + (i * block + base)
        table[pl.ds(pl.multiple_of(i * block, block), block), :] = jnp.where(
            slot == row, 1.0, 0.0
        ).astype(BF16)
        return carry

    lax.fori_loop(0, extent // block, step, 0)


def kernel(
    count,
    pos_hbm, vel_hbm, mass_hbm, lists_hbm, rim_hbm, pair_hbm, tiles_hbm,
    vel_out, lam_out,
    pos_in, vel_in, mass_in, lists_in, rim_in, pair_in, tiles_in,
    ends, tab0, tab1, tab2, rim_tab, slot_tab, edge_tab, tiles_hi, tiles_lo,
    send_a, send_k, send_r, send_c, send_f,
    recv_a, recv_l, recv_k, recv_r, recv_c, recv_f,
    in_sem, send_sem, recv_sem,
):
    grains = pos_in.shape[1]
    half = lists_in.shape[1]
    width = rim_in.shape[1]
    contacts = pair_in.shape[1]
    tiles, tile = tiles_in.shape[:2]
    bits = count.bit_length() - 1
    far, mid, near = (1 << (bits - 1 - level) for level in range(3))
    masks = (0, near, mid, mid | near)
    me = lax.axis_index("parts")
    high = me >= far
    low = me < far

    def shifted(base, by):
        return lax.rem(base + (by + count), count)

    def flipped(base, mask):
        return lax.bitwise_xor(base, jnp.int32(mask))

    def inside(by):
        return me >= -by if by < 0 else me < count - by

    loads = [
        pltpu.make_async_copy(src, dst, in_sem.at[i])
        for i, (src, dst) in enumerate(
            [
                (lists_hbm, lists_in), (pos_hbm, pos_in), (vel_hbm, vel_in), (mass_hbm, mass_in),
                (rim_hbm, rim_in), (pair_hbm, pair_in), (tiles_hbm, tiles_in),
            ]
        )
    ]
    for load in loads:
        load.start()

    barrier = pltpu.get_barrier_semaphore()

    def greet(peer):
        pl.semaphore_signal(barrier, inc=1, device_id=(peer,), device_id_type=MESH)

    @pl.when(low)
    def _():
        for mask in masks:
            greet(flipped(me, far | mask))

    for mask in masks[1:]:
        greet(flipped(me, mask))
    awaited = 3 + 4 * high.astype(jnp.int32)
    for by in (1, -1, 2, -2):
        pl.when(inside(by))(functools.partial(greet, shifted(me, by)))
        awaited += inside(by).astype(jnp.int32)

    routes = [(send_a, recv_a.at[k], flipped(me, far | masks[k]), 0) for k in range(4)]
    routes += [(lists_in, recv_l.at[k - 1], flipped(me, masks[k]), 0) for k in (1, 2, 3)]
    routes += [(send_k, recv_k.at[k - 1], flipped(me, masks[k]), 0) for k in (1, 2, 3)]
    routes += [
        (send_r, recv_r.at[0], shifted(me, 1), 1),
        (send_r, recv_r.at[1], shifted(me, -1), -1),
        (send_c.at[0], recv_c.at[0], shifted(me, 1), 1),
        (send_c.at[1], recv_c.at[1], shifted(me, -1), -1),
        (send_c.at[0], recv_c.at[2], shifted(me, 2), 2),
        (send_c.at[1], recv_c.at[3], shifted(me, -2), -2),
        (send_f.at[0], recv_f.at[0], shifted(me, 1), 1),
        (send_f.at[1], recv_f.at[1], shifted(me, -1), -1),
    ]
    copies = [
        pltpu.make_async_remote_copy(
            src_ref=src, dst_ref=dst, send_sem=send_sem.at[i], recv_sem=recv_sem.at[i],
            device_id=(target,), device_id_type=MESH,
        )
        for i, (src, dst, target, _) in enumerate(routes)
    ]

    def guarded(action, by):
        if by == 0:
            action()
        else:
            pl.when(inside(by))(action)

    def send(*which):
        for i in which:
            guarded(copies[i].start, routes[i][3])

    def receive(*which):
        for i in which:
            guarded(copies[i].wait_recv, -routes[i][3])

    def blank(*refs):
        for ref in refs:
            ref[...] = jnp.zeros(ref.shape, F32)

    for load in loads[:4]:
        load.wait()
    put_one_hot(tab0.at[0], lists_in[0:1, :])
    state = rows8(pos_in[...], vel_in[...], mass_in[...])
    send_a[...] = pick(state, tab0[0])

    pl.semaphore_wait(barrier, awaited)
    pl.when(high)(lambda: send(0, 1, 2, 3))
    send(4, 5, 6)
    ones = jnp.ones((8, half), F32)

    def keep(table):
        return 1.0 - spread(ones, table)[:1]

    kept = state * keep(tab0[0])
    send_k[...] = kept
    send(7, 8, 9)

    pl.when(me < 1)(lambda: blank(recv_r.at[0], recv_c.at[0], recv_f.at[0]))
    pl.when(me > count - 2)(lambda: blank(recv_r.at[1], recv_c.at[1], recv_f.at[1]))
    pl.when(me < 2)(lambda: blank(recv_c.at[2]))
    pl.when(me > count - 3)(lambda: blank(recv_c.at[3]))

    loads[4].wait()
    loads[5].wait()
    rim_row = rim_in[...]
    put_one_hot(tab1.at[0], lists_in[1:2, :])
    put_one_hot(tab2.at[0], lists_in[2:3, :])
    put_one_hot(rim_tab, rim_row)
    first, second = pair_in[0:1, :], pair_in[1:2, :]

    def touch(slot):
        return (jnp.where(slot == first, 1.0, 0.0) - jnp.where(slot == second, 1.0, 0.0)).astype(
            BF16
        )

    def put_ends(i, carry):
        slot = lax.broadcasted_iota(jnp.int32, (32, contacts), 0) + i * 32
        ends[pl.ds(pl.multiple_of(i * 32, 32), 32), :] = touch(slot)
        return carry

    extent = grains + 2 * width
    lax.fori_loop(0, extent // 32, put_ends, 0)
    across = lax.broadcasted_iota(jnp.int32, (width, width), 0) == lax.broadcasted_iota(
        jnp.int32, (width, width), 1
    )
    rim_column = jnp.sum(jnp.where(across, rim_row, 0), axis=1, keepdims=True)
    for i in range(0, width, 32):
        ends[extent + i : extent + i + 32, :] = touch(rim_column[i : i + 32])

    loads[6].wait()
    eye = lax.broadcasted_iota(jnp.int32, (tile, tile), 0) == lax.broadcasted_iota(
        jnp.int32, (tile, tile), 1
    )
    diags = []
    for t in range(tiles):
        block = tiles_in[t]
        head = block.astype(BF16)
        tiles_hi[t * tile : (t + 1) * tile, :] = head
        tiles_lo[t * tile : (t + 1) * tile, :] = (block - head.astype(F32)).astype(BF16)
        diags.append(jnp.sum(jnp.where(eye, block, 0.0), axis=0, keepdims=True))
    diag = jnp.concatenate(diags, axis=1)
    own_tile = lax.broadcasted_iota(jnp.int32, (tiles, contacts), 0) == (
        lax.broadcasted_iota(jnp.int32, (tiles, contacts), 1) // tile
    )

    def coupled(lam):
        table = jnp.concatenate(
            [lam[:, t * tile : (t + 1) * tile] for t in range(tiles)], axis=0
        )
        product = spread(table, tiles_hi[...]) + spread(table, tiles_lo[...])
        return jnp.sum(jnp.where(own_tile, product, 0.0), axis=0, keepdims=True)

    lam = jnp.zeros((1, contacts), F32)
    pull = coupled(lam)

    code_row = lax.broadcasted_iota(jnp.int32, (8, half), 0)
    order = lax.broadcasted_iota(jnp.int32, (8, half), 1).astype(F32) + 1.0

    def coded(k, rows):
        codes = spread(jnp.where(code_row == k, order, 0.0), tab0[k])
        return jnp.concatenate([rows, codes], axis=0)

    parts = [coded(0, kept)]
    for k in (1, 2, 3):
        receive(3 + k)
        put_one_hot(tab0.at[k], recv_l[k - 1, 0:1, :])
        put_one_hot(tab1.at[k], recv_l[k - 1, 1:2, :])
        if k == 1:
            put_one_hot(tab2.at[1], recv_l[0, 2:3, :])
        receive(6 + k)
        parts.append(coded(k, recv_k[k - 1]))
    pair = [
        parts[k] * keep(tab1[k]) + spread(pick(parts[k + 2], tab1[k + 2]), tab1[k])
        for k in (0, 1)
    ]
    state = pair[0] * keep(tab2[0]) + spread(pick(pair[1], tab2[1]), tab2[0])
    edge = pick(state, rim_tab[...])
    for k in range(4):
        put_one_hot(
            edge_tab.at[k * half : (k + 1) * half, :], edge[8 + k : 9 + k].astype(jnp.int32), 1
        )
        put_one_hot(
            slot_tab.at[k * half : (k + 1) * half, :], state[8 + k : 9 + k].astype(jnp.int32), 1
        )

    @pl.when(low)
    def _():
        for k in (2, 3, 1, 0):
            receive(k)
            send(k)

    pl.when(high)(lambda: receive(2, 3, 1, 0))
    arrived = split(jnp.concatenate([recv_a[k] for k in range(4)], axis=1))
    edge = edge[:8] + join(jnp.dot(arrived, edge_tab[...], preferred_element_type=F32))
    send_r[...] = edge
    send(10, 11)
    state = state[:8] + join(jnp.dot(arrived, slot_tab[...], preferred_element_type=F32))
    vel, mass = state[3:6], state[6:7]
    gathered = pick(state, ends[:grains, :])

    receive(10, 11)
    left, right = recv_r[0], recv_r[1]
    gathered += pick(jnp.concatenate([left, right], axis=1), ends[grains:extent, :])
    normal = gathered[0:3]
    speed = jnp.sum(normal * gathered[3:6], axis=0, keepdims=True)
    lam = jnp.maximum(0.0, lam - (pull + speed) / diag)
    force = rows8(normal * lam)
    partial = spread(force, ends[grains:, :])[0:3]
    ghost_left, ghost_right = partial[:, :width], partial[:, width : 2 * width]
    at_rim = partial[:, 2 * width :]
    send_c[0] = rows8(ghost_right, at_rim)
    send_c[1] = rows8(ghost_left, at_rim)
    send(12, 13, 14, 15)
    local = spread(force, ends[:grains, :])[0:3]
    base = pick(rows8(vel + mass * local), ends[:grains, :])[0:3]
    pull = coupled(lam)

    receive(12, 13, 14, 15)
    incoming = edge[6:7] * (recv_c[0, 0:3] + recv_c[1, 0:3])
    fresh_left = left[3:6] + left[6:7] * (recv_c[0, 3:6] + ghost_left + recv_c[2, 0:3])
    fresh_right = right[3:6] + right[6:7] * (recv_c[1, 3:6] + ghost_right + recv_c[3, 0:3])
    relative = base + pick(
        rows8(jnp.concatenate([fresh_left, fresh_right, incoming], axis=1)), ends[grains:, :]
    )[0:3]
    speed = jnp.sum(normal * relative, axis=0, keepdims=True)
    lam = jnp.maximum(0.0, lam - (pull + speed) / diag)
    force = rows8(normal * lam)
    partial = spread(force, ends[grains:extent, :])
    send_f[0] = partial[:, width:]
    send_f[1] = partial[:, :width]
    send(16, 17)
    lam_out[...] = lam
    base = vel + mass * spread(force, ends[:grains, :])[0:3]

    receive(16, 17)
    vel_out[...] = base + mass * spread(recv_f[0] + recv_f[1], rim_tab[...])[0:3]
    for i in range(MESSAGES):
        guarded(copies[i].wait_send, routes[i][3])


def body(count, positions, velocity, inv_mass, swap_lists, rim_list, contact_pair, delassus):
    grains = positions.shape[1]
    half = swap_lists.shape[1]
    width = rim_list.shape[0]
    contacts = contact_pair.shape[1]
    tiles, tile = delassus.shape[:2]
    args = (
        positions, velocity, inv_mass.reshape(1, grains), swap_lists, rim_list.reshape(1, width),
        contact_pair, delassus,
    )
    args = tuple(pltpu.with_memory_space_constraint(arg, pltpu.HBM) for arg in args)

    current, lam = pl.pallas_call(
        lambda *refs: kernel(count, *refs),
        out_shape=(
            jax.ShapeDtypeStruct((3, grains), F32),
            jax.ShapeDtypeStruct((1, contacts), F32),
        ),
        in_specs=[pl.BlockSpec(memory_space=pltpu.HBM)] * len(args),
        out_specs=(
            pl.BlockSpec(memory_space=pltpu.VMEM),
            pl.BlockSpec(memory_space=pltpu.VMEM),
        ),
        scratch_shapes=[pltpu.VMEM(arg.shape, arg.dtype) for arg in args]
        + [
            pltpu.VMEM((grains + 3 * width, contacts), BF16),
            pltpu.VMEM((4, grains, half), BF16),
            pltpu.VMEM((4, grains, half), BF16),
            pltpu.VMEM((2, grains, half), BF16),
            pltpu.VMEM((grains, width), BF16),
            pltpu.VMEM((4 * half, grains), BF16),
            pltpu.VMEM((4 * half, width), BF16),
            pltpu.VMEM((contacts, tile), BF16),
            pltpu.VMEM((contacts, tile), BF16),
            pltpu.VMEM((8, half), F32),
            pltpu.VMEM((8, grains), F32),
            pltpu.VMEM((8, width), F32),
            pltpu.VMEM((2, 8, width), F32),
            pltpu.VMEM((2, 8, width), F32),
            pltpu.VMEM((4, 8, half), F32),
            pltpu.VMEM((3, 3, half), jnp.int32),
            pltpu.VMEM((3, 8, grains), F32),
            pltpu.VMEM((2, 8, width), F32),
            pltpu.VMEM((4, 8, width), F32),
            pltpu.VMEM((2, 8, width), F32),
            pltpu.SemaphoreType.DMA((len(args),)),
            pltpu.SemaphoreType.DMA((MESSAGES,)),
            pltpu.SemaphoreType.DMA((MESSAGES,)),
        ],
        compiler_params=pltpu.CompilerParams(
            collective_id=0, has_side_effects=True, vmem_limit_bytes=32 << 20
        ),
        name="contact_step",
    )(*args)
    return current, lam.reshape(contacts)


def solution(mesh):
    count = mesh.shape["parts"]
    in_specs = (
        P(None, "parts"),
        P(None, "parts"),
        P("parts"),
        P(None, "parts"),
        P("parts"),
        P(None, "parts"),
        P("parts", None, None),
    )
    out_specs = (P(None, "parts"), P("parts"))
    return jax.shard_map(
        lambda *args: body(count, *args),
        mesh=mesh, in_specs=in_specs, out_specs=out_specs, check_vma=False,
    )
```

```python
import functools

import jax
import jax.numpy as jnp
from jax import lax
from jax.experimental import pallas as pl
from jax.experimental.pallas import tpu as pltpu
from jax.sharding import PartitionSpec as P

MESH = pl.DeviceIdType.MESH
F32 = jnp.float32
BF16 = jnp.bfloat16
MESSAGES = 18


def split(x):
    head = x.astype(BF16).astype(F32)
    return jnp.concatenate([head, x - head], axis=0).astype(BF16)


def join(y):
    half = y.shape[0] // 2
    return y[:half] + y[half:]


def pick(x, table):
    return join(jnp.dot(split(x), table, preferred_element_type=F32))


def spread(x, table):
    return join(
        lax.dot_general(split(x), table, (((1,), (1,)), ((), ())), preferred_element_type=F32)
    )


def rows8(*pieces):
    have = sum(piece.shape[0] for piece in pieces)
    if have < 8:
        pieces += (jnp.zeros((8 - have, pieces[0].shape[1]), F32),)
    return jnp.concatenate(pieces, axis=0)


def put_one_hot(table, row, base=0):
    extent, width = table.shape
    block = 64

    def step(i, carry):
        slot = lax.broadcasted_iota(jnp.int32, (block, width), 0) + (i * block + base)
        table[pl.ds(pl.multiple_of(i * block, block), block), :] = jnp.where(
            slot == row, 1.0, 0.0
        ).astype(BF16)
        return carry

    lax.fori_loop(0, extent // block, step, 0)


def kernel(
    count,
    pos_hbm, vel_hbm, mass_hbm, lists_hbm, rim_hbm, pair_hbm, tiles_hbm,
    vel_out, lam_out,
    pos_in, vel_in, mass_in, lists_in, rim_in, pair_in, tiles_in,
    ends, tab0, tab1, tab2, rim_tab, slot_tab, edge_tab, tiles_hi, tiles_lo,
    send_a, send_k, send_r, send_c, send_f,
    recv_a, recv_l, recv_k, recv_r, recv_c, recv_f,
    in_sem, send_sem, recv_sem, far_sem,
):
    grains = pos_in.shape[1]
    half = lists_in.shape[1]
    width = rim_in.shape[1]
    contacts = pair_in.shape[1]
    tiles, tile = tiles_in.shape[:2]
    bits = count.bit_length() - 1
    far, mid, near = (1 << (bits - 1 - level) for level in range(3))
    masks = (0, near, mid, mid | near)
    me = lax.axis_index("parts")
    high = me >= far
    low = me < far

    def shifted(base, by):
        return lax.rem(base + (by + count), count)

    def flipped(base, mask):
        return lax.bitwise_xor(base, jnp.int32(mask))

    def inside(by):
        return me >= -by if by < 0 else me < count - by

    loads = [
        pltpu.make_async_copy(src, dst, in_sem.at[i])
        for i, (src, dst) in enumerate(
            [
                (lists_hbm, lists_in), (pos_hbm, pos_in), (vel_hbm, vel_in), (mass_hbm, mass_in),
                (rim_hbm, rim_in), (pair_hbm, pair_in), (tiles_hbm, tiles_in),
            ]
        )
    ]
    for load in loads:
        load.start()

    barrier = pltpu.get_barrier_semaphore()

    def greet(peer):
        pl.semaphore_signal(barrier, inc=1, device_id=(peer,), device_id_type=MESH)

    @pl.when(low)
    def _():
        for mask in masks:
            greet(flipped(me, far | mask))

    for mask in (near, mid):
        greet(flipped(me, mask))
    pl.when(low)(lambda: greet(flipped(me, masks[3])))
    awaited = 3 + 3 * high.astype(jnp.int32)
    for by in (1, -1):
        pl.when(inside(by))(functools.partial(greet, shifted(me, by)))
        awaited += inside(by).astype(jnp.int32)

    routes = [(send_a, recv_a.at[k], flipped(me, far | masks[k]), 0) for k in range(4)]
    routes += [(lists_in, recv_l.at[k - 1], flipped(me, masks[k]), 0) for k in (1, 2, 3)]
    routes += [(send_k, recv_k.at[k - 1], flipped(me, masks[k]), 0) for k in (1, 2, 3)]
    routes += [
        (send_r, recv_r.at[0], shifted(me, 1), 1),
        (send_r, recv_r.at[1], shifted(me, -1), -1),
        (send_c.at[0], recv_c.at[0], shifted(me, 1), 1),
        (send_c.at[1], recv_c.at[1], shifted(me, -1), -1),
        (send_c.at[0], recv_c.at[2], shifted(me, 2), 2),
        (send_c.at[1], recv_c.at[3], shifted(me, -2), -2),
        (send_f.at[0], recv_f.at[0], shifted(me, 1), 1),
        (send_f.at[1], recv_f.at[1], shifted(me, -1), -1),
    ]
    copies = [
        pltpu.make_async_remote_copy(
            src_ref=src, dst_ref=dst, send_sem=send_sem.at[i], recv_sem=recv_sem.at[i],
            device_id=(target,), device_id_type=MESH,
        )
        for i, (src, dst, target, _) in enumerate(routes)
    ]

    def guarded(action, by):
        if by == 0:
            action()
        else:
            pl.when(inside(by))(action)

    def send(*which):
        for i in which:
            guarded(copies[i].start, routes[i][3])

    def receive(*which):
        for i in which:
            guarded(copies[i].wait_recv, -routes[i][3])

    def blank(*refs):
        for ref in refs:
            ref[...] = jnp.zeros(ref.shape, F32)

    for load in loads[:4]:
        load.wait()
    put_one_hot(tab0.at[0], lists_in[0:1, :])
    state = rows8(pos_in[...], vel_in[...], mass_in[...])
    send_a[...] = pick(state, tab0[0])

    pl.semaphore_wait(barrier, awaited)

    @pl.when(high)
    def _():
        for k in range(4):
            pl.semaphore_signal(
                far_sem.at[k], inc=1, device_id=(routes[k][2],), device_id_type=MESH
            )
        send(0, 1, 2, 3)

    send(4, 5)
    pl.when(low)(lambda: send(6))
    ones = jnp.ones((8, half), F32)

    def keep(table):
        return 1.0 - spread(ones, table)[:1]

    kept = state * keep(tab0[0])
    send_k[...] = kept
    send(7, 8)
    pl.when(low)(lambda: send(9))

    @pl.when(high)
    def _():
        receive(4)
        send(6, 9)

    pl.when(me < 1)(lambda: blank(recv_r.at[0], recv_c.at[0], recv_f.at[0]))
    pl.when(me > count - 2)(lambda: blank(recv_r.at[1], recv_c.at[1], recv_f.at[1]))
    pl.when(me < 2)(lambda: blank(recv_c.at[2]))
    pl.when(me > count - 3)(lambda: blank(recv_c.at[3]))

    loads[4].wait()
    loads[5].wait()
    rim_row = rim_in[...]
    put_one_hot(tab1.at[0], lists_in[1:2, :])
    put_one_hot(tab2.at[0], lists_in[2:3, :])
    put_one_hot(rim_tab, rim_row)
    first, second = pair_in[0:1, :], pair_in[1:2, :]

    def touch(slot):
        return (jnp.where(slot == first, 1.0, 0.0) - jnp.where(slot == second, 1.0, 0.0)).astype(
            BF16
        )

    def put_ends(i, carry):
        slot = lax.broadcasted_iota(jnp.int32, (32, contacts), 0) + i * 32
        ends[pl.ds(pl.multiple_of(i * 32, 32), 32), :] = touch(slot)
        return carry

    extent = grains + 2 * width
    lax.fori_loop(0, extent // 32, put_ends, 0)
    across = lax.broadcasted_iota(jnp.int32, (width, width), 0) == lax.broadcasted_iota(
        jnp.int32, (width, width), 1
    )
    rim_column = jnp.sum(jnp.where(across, rim_row, 0), axis=1, keepdims=True)
    for i in range(0, width, 32):
        ends[extent + i : extent + i + 32, :] = touch(rim_column[i : i + 32])

    loads[6].wait()
    eye = lax.broadcasted_iota(jnp.int32, (tile, tile), 0) == lax.broadcasted_iota(
        jnp.int32, (tile, tile), 1
    )
    diags = []
    for t in range(tiles):
        block = tiles_in[t]
        head = block.astype(BF16)
        tiles_hi[t * tile : (t + 1) * tile, :] = head
        tiles_lo[t * tile : (t + 1) * tile, :] = (block - head.astype(F32)).astype(BF16)
        diags.append(jnp.sum(jnp.where(eye, block, 0.0), axis=0, keepdims=True))
    diag = jnp.concatenate(diags, axis=1)
    own_tile = lax.broadcasted_iota(jnp.int32, (tiles, contacts), 0) == (
        lax.broadcasted_iota(jnp.int32, (tiles, contacts), 1) // tile
    )

    def coupled(lam):
        table = jnp.concatenate(
            [lam[:, t * tile : (t + 1) * tile] for t in range(tiles)], axis=0
        )
        product = spread(table, tiles_hi[...]) + spread(table, tiles_lo[...])
        return jnp.sum(jnp.where(own_tile, product, 0.0), axis=0, keepdims=True)

    lam = jnp.zeros((1, contacts), F32)
    pull = coupled(lam)

    code_row = lax.broadcasted_iota(jnp.int32, (8, half), 0)
    order = lax.broadcasted_iota(jnp.int32, (8, half), 1).astype(F32) + 1.0

    def coded(k, rows):
        codes = spread(jnp.where(code_row == k, order, 0.0), tab0[k])
        return jnp.concatenate([rows, codes], axis=0)

    parts = [coded(0, kept)]
    pl.when(low)(lambda: receive(4))
    for k in (1, 2, 3):
        if k > 1:
            receive(3 + k)
        put_one_hot(tab0.at[k], recv_l[k - 1, 0:1, :])
        put_one_hot(tab1.at[k], recv_l[k - 1, 1:2, :])
        if k == 1:
            put_one_hot(tab2.at[1], recv_l[0, 2:3, :])
        receive(6 + k)
        parts.append(coded(k, recv_k[k - 1]))
    pair = [
        parts[k] * keep(tab1[k]) + spread(pick(parts[k + 2], tab1[k + 2]), tab1[k])
        for k in (0, 1)
    ]
    state = pair[0] * keep(tab2[0]) + spread(pick(pair[1], tab2[1]), tab2[0])
    edge = pick(state, rim_tab[...])
    for k in range(4):
        put_one_hot(
            edge_tab.at[k * half : (k + 1) * half, :], edge[8 + k : 9 + k].astype(jnp.int32), 1
        )
        put_one_hot(
            slot_tab.at[k * half : (k + 1) * half, :], state[8 + k : 9 + k].astype(jnp.int32), 1
        )

    @pl.when(low)
    def _():
        for k in range(4):
            pl.semaphore_wait(far_sem.at[k], 1)
            send(k)

    receive(2, 3, 1, 0)
    arrived = split(jnp.concatenate([recv_a[k] for k in range(4)], axis=1))
    edge = edge[:8] + join(jnp.dot(arrived, edge_tab[...], preferred_element_type=F32))
    send_r[...] = edge
    send(10, 11)
    state = state[:8] + join(jnp.dot(arrived, slot_tab[...], preferred_element_type=F32))
    vel, mass = state[3:6], state[6:7]
    gathered = pick(state, ends[:grains, :])

    receive(10, 11)
    left, right = recv_r[0], recv_r[1]
    gathered += pick(jnp.concatenate([left, right], axis=1), ends[grains:extent, :])
    normal = gathered[0:3]
    speed = jnp.sum(normal * gathered[3:6], axis=0, keepdims=True)
    lam = jnp.maximum(0.0, lam - (pull + speed) / diag)
    force = rows8(normal * lam)
    partial = spread(force, ends[grains:, :])[0:3]
    ghost_left, ghost_right = partial[:, :width], partial[:, width : 2 * width]
    at_rim = partial[:, 2 * width :]
    send_c[0] = rows8(ghost_right, at_rim)
    send_c[1] = rows8(ghost_left, at_rim)
    send(12, 13, 14, 15)
    local = spread(force, ends[:grains, :])[0:3]
    base = pick(rows8(vel + mass * local), ends[:grains, :])[0:3]
    pull = coupled(lam)

    receive(12, 13, 14, 15)
    incoming = edge[6:7] * (recv_c[0, 0:3] + recv_c[1, 0:3])
    fresh_left = left[3:6] + left[6:7] * (recv_c[0, 3:6] + ghost_left + recv_c[2, 0:3])
    fresh_right = right[3:6] + right[6:7] * (recv_c[1, 3:6] + ghost_right + recv_c[3, 0:3])
    relative = base + pick(
        rows8(jnp.concatenate([fresh_left, fresh_right, incoming], axis=1)), ends[grains:, :]
    )[0:3]
    speed = jnp.sum(normal * relative, axis=0, keepdims=True)
    lam = jnp.maximum(0.0, lam - (pull + speed) / diag)
    force = rows8(normal * lam)
    partial = spread(force, ends[grains:extent, :])
    send_f[0] = partial[:, width:]
    send_f[1] = partial[:, :width]
    send(16, 17)
    lam_out[...] = lam
    base = vel + mass * spread(force, ends[:grains, :])[0:3]

    receive(16, 17)
    vel_out[...] = base + mass * spread(recv_f[0] + recv_f[1], rim_tab[...])[0:3]
    for i in range(MESSAGES):
        guarded(copies[i].wait_send, routes[i][3])


def body(count, positions, velocity, inv_mass, swap_lists, rim_list, contact_pair, delassus):
    grains = positions.shape[1]
    half = swap_lists.shape[1]
    width = rim_list.shape[0]
    contacts = contact_pair.shape[1]
    tiles, tile = delassus.shape[:2]
    args = (
        positions, velocity, inv_mass.reshape(1, grains), swap_lists, rim_list.reshape(1, width),
        contact_pair, delassus,
    )
    args = tuple(pltpu.with_memory_space_constraint(arg, pltpu.HBM) for arg in args)

    current, lam = pl.pallas_call(
        lambda *refs: kernel(count, *refs),
        out_shape=(
            jax.ShapeDtypeStruct((3, grains), F32),
            jax.ShapeDtypeStruct((1, contacts), F32),
        ),
        in_specs=[pl.BlockSpec(memory_space=pltpu.HBM)] * len(args),
        out_specs=(
            pl.BlockSpec(memory_space=pltpu.VMEM),
            pl.BlockSpec(memory_space=pltpu.VMEM),
        ),
        scratch_shapes=[pltpu.VMEM(arg.shape, arg.dtype) for arg in args]
        + [
            pltpu.VMEM((grains + 3 * width, contacts), BF16),
            pltpu.VMEM((4, grains, half), BF16),
            pltpu.VMEM((4, grains, half), BF16),
            pltpu.VMEM((2, grains, half), BF16),
            pltpu.VMEM((grains, width), BF16),
            pltpu.VMEM((4 * half, grains), BF16),
            pltpu.VMEM((4 * half, width), BF16),
            pltpu.VMEM((contacts, tile), BF16),
            pltpu.VMEM((contacts, tile), BF16),
            pltpu.VMEM((8, half), F32),
            pltpu.VMEM((8, grains), F32),
            pltpu.VMEM((8, width), F32),
            pltpu.VMEM((2, 8, width), F32),
            pltpu.VMEM((2, 8, width), F32),
            pltpu.VMEM((4, 8, half), F32),
            pltpu.VMEM((3, 3, half), jnp.int32),
            pltpu.VMEM((3, 8, grains), F32),
            pltpu.VMEM((2, 8, width), F32),
            pltpu.VMEM((4, 8, width), F32),
            pltpu.VMEM((2, 8, width), F32),
            pltpu.SemaphoreType.DMA((len(args),)),
            pltpu.SemaphoreType.DMA((MESSAGES,)),
            pltpu.SemaphoreType.DMA((MESSAGES,)),
            pltpu.SemaphoreType.REGULAR((4,)),
        ],
        compiler_params=pltpu.CompilerParams(
            collective_id=0, has_side_effects=True, vmem_limit_bytes=32 << 20
        ),
        name="contact_step",
    )(*args)
    return current, lam.reshape(contacts)


def solution(mesh):
    count = mesh.shape["parts"]
    in_specs = (
        P(None, "parts"),
        P(None, "parts"),
        P("parts"),
        P(None, "parts"),
        P("parts"),
        P(None, "parts"),
        P("parts", None, None),
    )
    out_specs = (P(None, "parts"), P("parts"))
    return jax.shard_map(
        lambda *args: body(count, *args),
        mesh=mesh, in_specs=in_specs, out_specs=out_specs, check_vma=False,
    )
```

```python
import functools

import jax
import jax.numpy as jnp
from jax import lax
from jax.experimental import pallas as pl
from jax.experimental.pallas import tpu as pltpu
from jax.sharding import PartitionSpec as P

MESH = pl.DeviceIdType.MESH
F32 = jnp.float32
BF16 = jnp.bfloat16
MESSAGES = 28


def split(x):
    head = x.astype(BF16).astype(F32)
    return jnp.concatenate([head, x - head], axis=0).astype(BF16)


def join(y):
    half = y.shape[0] // 2
    return y[:half] + y[half:]


def pick(x, table):
    return join(jnp.dot(split(x), table, preferred_element_type=F32))


def spread(x, table):
    return join(
        lax.dot_general(split(x), table, (((1,), (1,)), ((), ())), preferred_element_type=F32)
    )


def rows8(*pieces):
    have = sum(piece.shape[0] for piece in pieces)
    if have < 8:
        pieces += (jnp.zeros((8 - have, pieces[0].shape[1]), F32),)
    return jnp.concatenate(pieces, axis=0)


def put_one_hot(table, row, base=0):
    extent, width = table.shape
    block = 64

    def step(i, carry):
        slot = lax.broadcasted_iota(jnp.int32, (block, width), 0) + (i * block + base)
        table[pl.ds(pl.multiple_of(i * block, block), block), :] = jnp.where(
            slot == row, 1.0, 0.0
        ).astype(BF16)
        return carry

    lax.fori_loop(0, extent // block, step, 0)


def kernel(
    count,
    pos_hbm, vel_hbm, mass_hbm, lists_hbm, rim_hbm, pair_hbm, tiles_hbm,
    vel_out, lam_out,
    pos_in, vel_in, mass_in, lists_in, rim_in, pair_in, tiles_in,
    ends, tab0, tab1, tab2, rim_tab, slot_tab, edge_tab, cross_tab, tiles_hi, tiles_lo,
    send_a, send_k, send_r, send_c, send_f, send_e,
    recv_a, recv_l, recv_k, recv_r, recv_c, recv_f, recv_x, recv_e, recv_p,
    in_sem, send_sem, recv_sem, far_sem, edge_sem, hail_sem, near_sem, seen_sem,
):
    grains = pos_in.shape[1]
    half = lists_in.shape[1]
    width = rim_in.shape[1]
    contacts = pair_in.shape[1]
    tiles, tile = tiles_in.shape[:2]
    bits = count.bit_length() - 1
    far, mid, near = (1 << (bits - 1 - level) for level in range(3))
    masks = (0, near, mid, mid | near)
    plane = count // 16
    me = lax.axis_index("parts")
    high = me >= far
    low = me < far

    def shifted(base, by):
        return lax.rem(base + (by + count), count)

    def flipped(base, mask):
        return lax.bitwise_xor(base, jnp.int32(mask))

    def both(*conditions):
        return functools.reduce(jnp.logical_and, conditions)

    def inside(by):
        return me >= -by if by < 0 else me < count - by

    spot = lax.rem(me, plane)
    top, bottom = spot == plane - 1, spot == 0
    edge_side = jnp.where(top, 1, -1)
    beyond = me + edge_side
    across = jnp.logical_and(
        jnp.logical_or(top, bottom), jnp.logical_and(beyond >= 0, beyond < count)
    )
    relays = [flipped(me, far | mask) + edge_side for mask in masks]
    relayed = [
        both(jnp.logical_or(both(top, high), bottom), to >= 0, to < count) for to in relays
    ]
    carrier = both(bottom, me > 0, me <= far)
    carries = [flipped(me - carrier.astype(jnp.int32), far | mask) + 1 for mask in masks]
    carried = [both(carrier, to < count) for to in carries]
    served = both(bottom, me > far)

    loads = [
        pltpu.make_async_copy(src, dst, in_sem.at[i])
        for i, (src, dst) in enumerate(
            [
                (lists_hbm, lists_in), (pos_hbm, pos_in), (vel_hbm, vel_in), (mass_hbm, mass_in),
                (rim_hbm, rim_in), (pair_hbm, pair_in), (tiles_hbm, tiles_in),
            ]
        )
    ]
    for load in loads:
        load.start()

    barrier = pltpu.get_barrier_semaphore()

    def greet(peer):
        pl.semaphore_signal(barrier, inc=1, device_id=(peer,), device_id_type=MESH)

    @pl.when(low)
    def _():
        for mask in masks:
            greet(flipped(me, far | mask))

    for mask in (near, mid):
        greet(flipped(me, mask))
    pl.when(low)(lambda: greet(flipped(me, masks[3])))
    awaited = 3 + 3 * high.astype(jnp.int32)
    lower, upper = both(bottom, across), both(top, across)
    for by, skipped, excused in ((1, upper, False), (-1, False, lower)):
        pl.when(both(inside(by), jnp.logical_not(skipped)))(
            functools.partial(greet, shifted(me, by))
        )
        awaited += both(inside(by), jnp.logical_not(excused)).astype(jnp.int32)
    hailing = both(upper, beyond >= far)
    awaited += 4 * hailing.astype(jnp.int32)
    hailed = [jnp.logical_and(jnp.logical_and(low, bottom), condition) for condition in relayed]
    for to, condition in zip(relays + carries, hailed + carried):
        pl.when(condition)(functools.partial(greet, to))
    awaited += 4 * served.astype(jnp.int32)

    @pl.when(jnp.logical_and(across, beyond < far))
    def _():
        for mask in masks:
            greet(flipped(beyond, far | mask))

    for condition in relayed:
        awaited += jnp.logical_and(high, condition).astype(jnp.int32)

    routes = [(send_a, recv_a.at[k], flipped(me, far | masks[k]), None, None) for k in range(4)]
    routes += [
        (src, dst.at[k - 1], flipped(me, masks[k]), None, None)
        for src, dst in ((lists_in, recv_l), (send_k, recv_k))
        for k in (1, 2, 3)
    ]
    routes += [
        (src, dst, shifted(me, by), inside(by), inside(-by))
        for src, dst, by in (
            (send_r, recv_r.at[0], 1),
            (send_r, recv_r.at[1], -1),
            (send_c.at[0], recv_c.at[0], 1),
            (send_c.at[1], recv_c.at[1], -1),
            (send_c.at[0], recv_c.at[2], 2),
            (send_c.at[1], recv_c.at[3], -2),
            (send_f.at[0], recv_f.at[0], 1),
            (send_f.at[1], recv_f.at[1], -1),
        )
    ]
    for i, out_gate, in_gate in ((10, top, bottom), (11, bottom, top)):
        routes[i] = routes[i][:3] + tuple(
            jnp.logical_and(condition, jnp.logical_not(gate))
            for condition, gate in zip(routes[i][3:], (out_gate, in_gate))
        )
    direct = both(across, jnp.logical_not(served))
    routes += [(send_a, recv_x.at[k], relays[k], relayed[k], direct) for k in range(4)]
    routes += [(send_e, recv_e, beyond, across, across)]
    routes += [(send_a, recv_p, beyond, both(top, low), carrier)]
    routes += [(recv_p, recv_x.at[k], carries[k], carried[k], served) for k in range(4)]
    copies = [
        pltpu.make_async_remote_copy(
            src_ref=src, dst_ref=dst, send_sem=send_sem.at[i], recv_sem=recv_sem.at[i],
            device_id=(target,), device_id_type=MESH,
        )
        for i, (src, dst, target, _, _) in enumerate(routes)
    ]

    def guarded(action, condition):
        if condition is None:
            action()
        else:
            pl.when(condition)(action)

    def send(*which):
        for i in which:
            guarded(copies[i].start, routes[i][3])

    def receive(*which):
        for i in which:
            guarded(copies[i].wait_recv, routes[i][4])

    def blank(*refs):
        for ref in refs:
            ref[...] = jnp.zeros(ref.shape, F32)

    for load in loads[:4]:
        load.wait()
    put_one_hot(tab0.at[0], lists_in[0:1, :])
    state = rows8(pos_in[...], vel_in[...], mass_in[...])
    send_a[...] = pick(state, tab0[0])

    pl.semaphore_wait(barrier, awaited)

    def tell(semaphore, peer):
        pl.semaphore_signal(semaphore, inc=1, device_id=(peer,), device_id_type=MESH)

    @pl.when(high)
    def _():
        for k in range(4):
            tell(far_sem.at[k], routes[k][2])
        tell(near_sem, flipped(me, near))
        send(18, 19, 20, 21, 0, 1, 2, 3)

    pl.when(upper)(lambda: tell(seen_sem, beyond))

    send(23)

    @pl.when(hailing)
    def _():
        for k in range(4):
            tell(edge_sem.at[k], flipped(beyond, far | masks[k]))

    @pl.when(served)
    def _():
        for k in range(4):
            tell(hail_sem.at[k], flipped(me - 1, far | masks[k]) + 1)

    send(4, 5)
    pl.when(low)(lambda: send(6))
    ones = jnp.ones((8, half), F32)

    def keep(table):
        return 1.0 - spread(ones, table)[:1]

    kept = state * keep(tab0[0])
    send_k[...] = kept
    send(7, 8)
    pl.when(low)(lambda: send(9))

    @pl.when(high)
    def _():
        pl.semaphore_wait(near_sem, 1)
        send(6, 9)

    pl.when(me < 1)(lambda: blank(recv_r.at[0], recv_c.at[0], recv_f.at[0]))
    pl.when(me > count - 2)(lambda: blank(recv_r.at[1], recv_c.at[1], recv_f.at[1]))
    pl.when(me < 2)(lambda: blank(recv_c.at[2]))
    pl.when(me > count - 3)(lambda: blank(recv_c.at[3]))

    loads[4].wait()
    loads[5].wait()
    rim_row = rim_in[...]
    put_one_hot(tab1.at[0], lists_in[1:2, :])
    put_one_hot(tab2.at[0], lists_in[2:3, :])
    put_one_hot(rim_tab, rim_row)
    first, second = pair_in[0:1, :], pair_in[1:2, :]

    def touch(slot):
        return (jnp.where(slot == first, 1.0, 0.0) - jnp.where(slot == second, 1.0, 0.0)).astype(
            BF16
        )

    def put_ends(i, carry):
        slot = lax.broadcasted_iota(jnp.int32, (32, contacts), 0) + i * 32
        ends[pl.ds(pl.multiple_of(i * 32, 32), 32), :] = touch(slot)
        return carry

    extent = grains + 2 * width
    lax.fori_loop(0, extent // 32, put_ends, 0)
    square = lax.broadcasted_iota(jnp.int32, (width, width), 0) == lax.broadcasted_iota(
        jnp.int32, (width, width), 1
    )
    rim_column = jnp.sum(jnp.where(square, rim_row, 0), axis=1, keepdims=True)
    for i in range(0, width, 32):
        ends[extent + i : extent + i + 32, :] = touch(rim_column[i : i + 32])

    loads[6].wait()
    eye = lax.broadcasted_iota(jnp.int32, (tile, tile), 0) == lax.broadcasted_iota(
        jnp.int32, (tile, tile), 1
    )
    diags = []
    for t in range(tiles):
        block = tiles_in[t]
        head = block.astype(BF16)
        tiles_hi[t * tile : (t + 1) * tile, :] = head
        tiles_lo[t * tile : (t + 1) * tile, :] = (block - head.astype(F32)).astype(BF16)
        diags.append(jnp.sum(jnp.where(eye, block, 0.0), axis=0, keepdims=True))
    diag = jnp.concatenate(diags, axis=1)
    own_tile = lax.broadcasted_iota(jnp.int32, (tiles, contacts), 0) == (
        lax.broadcasted_iota(jnp.int32, (tiles, contacts), 1) // tile
    )

    def coupled(lam):
        table = jnp.concatenate(
            [lam[:, t * tile : (t + 1) * tile] for t in range(tiles)], axis=0
        )
        product = spread(table, tiles_hi[...]) + spread(table, tiles_lo[...])
        return jnp.sum(jnp.where(own_tile, product, 0.0), axis=0, keepdims=True)

    lam = jnp.zeros((1, contacts), F32)
    pull = coupled(lam)

    code_row = lax.broadcasted_iota(jnp.int32, (8, half), 0)
    order = lax.broadcasted_iota(jnp.int32, (8, half), 1).astype(F32) + 1.0

    def coded(k, rows):
        codes = spread(jnp.where(code_row == k, order, 0.0), tab0[k])
        return jnp.concatenate([rows, codes], axis=0)

    def answer():
        for k in range(4):
            pl.semaphore_wait(far_sem.at[k], 1)
            send(k)

    def carry():
        receive(23)
        for k in range(4):

            @pl.when(carried[k])
            def _():
                pl.semaphore_wait(hail_sem.at[k], 1)
                copies[24 + k].start()

    pl.when(both(low, me >= far // 2))(answer)
    pl.when(both(carrier, me >= far // 2))(carry)
    parts = [coded(0, kept)]
    for k in (1, 2, 3):
        receive(3 + k)
        put_one_hot(tab0.at[k], recv_l[k - 1, 0:1, :])
        put_one_hot(tab1.at[k], recv_l[k - 1, 1:2, :])
        if k == 1:
            put_one_hot(tab2.at[1], recv_l[0, 2:3, :])
        receive(6 + k)
        parts.append(coded(k, recv_k[k - 1]))
    pair = [
        parts[k] * keep(tab1[k]) + spread(pick(parts[k + 2], tab1[k + 2]), tab1[k])
        for k in (0, 1)
    ]
    state = pair[0] * keep(tab2[0]) + spread(pick(pair[1], tab2[1]), tab2[0])
    edge = pick(state, rim_tab[...])
    send_e[...] = edge
    pl.when(lower)(lambda: pl.semaphore_wait(seen_sem, 1))
    send(22)
    for k in range(4):
        put_one_hot(
            edge_tab.at[k * half : (k + 1) * half, :], edge[8 + k : 9 + k].astype(jnp.int32), 1
        )
        put_one_hot(
            slot_tab.at[k * half : (k + 1) * half, :], state[8 + k : 9 + k].astype(jnp.int32), 1
        )

    pl.when(me < far // 2)(answer)
    pl.when(both(carrier, me < far // 2))(carry)
    for k in range(4):

        @pl.when(hailed[k])
        def _():
            pl.semaphore_wait(edge_sem.at[k], 1)
            copies[18 + k].start()

    receive(2, 3, 1, 0)
    arrived = split(jnp.concatenate([recv_a[k] for k in range(4)], axis=1))
    edge = edge[:8] + join(jnp.dot(arrived, edge_tab[...], preferred_element_type=F32))
    send_r[...] = edge
    send(10, 11)
    state = state[:8] + join(jnp.dot(arrived, slot_tab[...], preferred_element_type=F32))
    vel, mass = state[3:6], state[6:7]
    gathered = pick(state, ends[:grains, :])

    @pl.when(across)
    def _():
        receive(22)
        for k in range(4):
            put_one_hot(
                cross_tab.at[k * half : (k + 1) * half, :],
                recv_e[8 + k : 9 + k, :].astype(jnp.int32), 1,
            )
        receive(20, 21, 19, 18, 26, 27, 25, 24)
        seen = split(jnp.concatenate([recv_x[k] for k in range(4)], axis=1))
        recv_r[top.astype(jnp.int32)] = recv_e[:8] + join(
            jnp.dot(seen, cross_tab[...], preferred_element_type=F32)
        )

    receive(10, 11)
    left, right = recv_r[0], recv_r[1]
    gathered += pick(jnp.concatenate([left, right], axis=1), ends[grains:extent, :])
    normal = gathered[0:3]
    speed = jnp.sum(normal * gathered[3:6], axis=0, keepdims=True)
    lam = jnp.maximum(0.0, lam - (pull + speed) / diag)
    force = rows8(normal * lam)
    partial = spread(force, ends[grains:, :])[0:3]
    ghost_left, ghost_right = partial[:, :width], partial[:, width : 2 * width]
    at_rim = partial[:, 2 * width :]
    send_c[0] = rows8(ghost_right, at_rim)
    send_c[1] = rows8(ghost_left, at_rim)
    send(12, 13, 14, 15)
    local = spread(force, ends[:grains, :])[0:3]
    base = pick(rows8(vel + mass * local), ends[:grains, :])[0:3]
    pull = coupled(lam)

    receive(12, 13, 14, 15)
    incoming = edge[6:7] * (recv_c[0, 0:3] + recv_c[1, 0:3])
    fresh_left = left[3:6] + left[6:7] * (recv_c[0, 3:6] + ghost_left + recv_c[2, 0:3])
    fresh_right = right[3:6] + right[6:7] * (recv_c[1, 3:6] + ghost_right + recv_c[3, 0:3])
    relative = base + pick(
        rows8(jnp.concatenate([fresh_left, fresh_right, incoming], axis=1)), ends[grains:, :]
    )[0:3]
    speed = jnp.sum(normal * relative, axis=0, keepdims=True)
    lam = jnp.maximum(0.0, lam - (pull + speed) / diag)
    force = rows8(normal * lam)
    partial = spread(force, ends[grains:extent, :])
    send_f[0] = partial[:, width:]
    send_f[1] = partial[:, :width]
    send(16, 17)
    lam_out[...] = lam
    base = vel + mass * spread(force, ends[:grains, :])[0:3]

    receive(16, 17)
    vel_out[...] = base + mass * spread(recv_f[0] + recv_f[1], rim_tab[...])[0:3]
    for i in range(MESSAGES):
        guarded(copies[i].wait_send, routes[i][3])


def body(count, positions, velocity, inv_mass, swap_lists, rim_list, contact_pair, delassus):
    grains = positions.shape[1]
    half = swap_lists.shape[1]
    width = rim_list.shape[0]
    contacts = contact_pair.shape[1]
    tiles, tile = delassus.shape[:2]
    args = (
        positions, velocity, inv_mass.reshape(1, grains), swap_lists, rim_list.reshape(1, width),
        contact_pair, delassus,
    )
    args = tuple(pltpu.with_memory_space_constraint(arg, pltpu.HBM) for arg in args)

    current, lam = pl.pallas_call(
        lambda *refs: kernel(count, *refs),
        out_shape=(
            jax.ShapeDtypeStruct((3, grains), F32),
            jax.ShapeDtypeStruct((1, contacts), F32),
        ),
        in_specs=[pl.BlockSpec(memory_space=pltpu.HBM)] * len(args),
        out_specs=(
            pl.BlockSpec(memory_space=pltpu.VMEM),
            pl.BlockSpec(memory_space=pltpu.VMEM),
        ),
        scratch_shapes=[pltpu.VMEM(arg.shape, arg.dtype) for arg in args]
        + [
            pltpu.VMEM((grains + 3 * width, contacts), BF16),
            pltpu.VMEM((4, grains, half), BF16),
            pltpu.VMEM((4, grains, half), BF16),
            pltpu.VMEM((2, grains, half), BF16),
            pltpu.VMEM((grains, width), BF16),
            pltpu.VMEM((4 * half, grains), BF16),
            pltpu.VMEM((4 * half, width), BF16),
            pltpu.VMEM((4 * half, width), BF16),
            pltpu.VMEM((contacts, tile), BF16),
            pltpu.VMEM((contacts, tile), BF16),
            pltpu.VMEM((8, half), F32),
            pltpu.VMEM((8, grains), F32),
            pltpu.VMEM((8, width), F32),
            pltpu.VMEM((2, 8, width), F32),
            pltpu.VMEM((2, 8, width), F32),
            pltpu.VMEM((16, width), F32),
            pltpu.VMEM((4, 8, half), F32),
            pltpu.VMEM((3, 3, half), jnp.int32),
            pltpu.VMEM((3, 8, grains), F32),
            pltpu.VMEM((2, 8, width), F32),
            pltpu.VMEM((4, 8, width), F32),
            pltpu.VMEM((2, 8, width), F32),
            pltpu.VMEM((4, 8, half), F32),
            pltpu.VMEM((16, width), F32),
            pltpu.VMEM((8, half), F32),
            pltpu.SemaphoreType.DMA((len(args),)),
            pltpu.SemaphoreType.DMA((MESSAGES,)),
            pltpu.SemaphoreType.DMA((MESSAGES,)),
            pltpu.SemaphoreType.REGULAR((4,)),
            pltpu.SemaphoreType.REGULAR((4,)),
            pltpu.SemaphoreType.REGULAR((4,)),
            pltpu.SemaphoreType.REGULAR,
            pltpu.SemaphoreType.REGULAR,
        ],
        compiler_params=pltpu.CompilerParams(
            collective_id=0, has_side_effects=True, vmem_limit_bytes=32 << 20
        ),
        name="contact_step",
    )(*args)
    return current, lam.reshape(contacts)


def solution(mesh):
    count = mesh.shape["parts"]
    in_specs = (
        P(None, "parts"),
        P(None, "parts"),
        P("parts"),
        P(None, "parts"),
        P("parts"),
        P(None, "parts"),
        P("parts", None, None),
    )
    out_specs = (P(None, "parts"), P("parts"))
    return jax.shard_map(
        lambda *args: body(count, *args),
        mesh=mesh, in_specs=in_specs, out_specs=out_specs, check_vma=False,
    )
```

```python
import functools

import jax
import jax.numpy as jnp
from jax import lax
from jax.experimental import pallas as pl
from jax.experimental.pallas import tpu as pltpu
from jax.sharding import PartitionSpec as P

MESH = pl.DeviceIdType.MESH
F32 = jnp.float32
BF16 = jnp.bfloat16
MESSAGES = 28


def split(x):
    head = x.astype(BF16).astype(F32)
    return jnp.concatenate([head, x - head], axis=0).astype(BF16)


def join(y):
    half = y.shape[0] // 2
    return y[:half] + y[half:]


def pick(x, table):
    return join(jnp.dot(split(x), table, preferred_element_type=F32))


def spread(x, table):
    return join(
        lax.dot_general(split(x), table, (((1,), (1,)), ((), ())), preferred_element_type=F32)
    )


def rows8(*pieces):
    have = sum(piece.shape[0] for piece in pieces)
    if have < 8:
        pieces += (jnp.zeros((8 - have, pieces[0].shape[1]), F32),)
    return jnp.concatenate(pieces, axis=0)


def put_one_hot(table, row, base=0):
    extent, width = table.shape
    block = 64

    def step(i, carry):
        slot = lax.broadcasted_iota(jnp.int32, (block, width), 0) + (i * block + base)
        table[pl.ds(pl.multiple_of(i * block, block), block), :] = jnp.where(
            slot == row, 1.0, 0.0
        ).astype(BF16)
        return carry

    lax.fori_loop(0, extent // block, step, 0)


def kernel(
    count,
    pos_hbm, vel_hbm, mass_hbm, lists_hbm, rim_hbm, pair_hbm, tiles_hbm,
    vel_out, lam_out,
    pos_in, vel_in, mass_in, lists_in, rim_in, pair_in, tiles_in,
    ends, tab0, tab1, tab2, rim_tab, slot_tab, edge_tab, cross_tab, tiles_hi, tiles_lo,
    send_a, send_k, send_r, send_c, send_f, send_e,
    recv_a, recv_l, recv_k, recv_r, recv_c, recv_f, recv_x, recv_e, recv_p,
    in_sem, send_sem, recv_sem, far_sem, edge_sem, hail_sem, near_sem, seen_sem,
):
    grains = pos_in.shape[1]
    half = lists_in.shape[1]
    width = rim_in.shape[1]
    contacts = pair_in.shape[1]
    tiles, tile = tiles_in.shape[:2]
    bits = count.bit_length() - 1
    far, mid, near = (1 << (bits - 1 - level) for level in range(3))
    masks = (0, near, mid, mid | near)
    plane = count // 16
    me = lax.axis_index("parts")
    high = me >= far
    low = me < far

    def shifted(base, by):
        return lax.rem(base + (by + count), count)

    def flipped(base, mask):
        return lax.bitwise_xor(base, jnp.int32(mask))

    def both(*conditions):
        return functools.reduce(jnp.logical_and, conditions)

    def inside(by):
        return me >= -by if by < 0 else me < count - by

    spot = lax.rem(me, plane)
    top, bottom = spot == plane - 1, spot == 0
    edge_side = jnp.where(top, 1, -1)
    beyond = me + edge_side
    across = jnp.logical_and(
        jnp.logical_or(top, bottom), jnp.logical_and(beyond >= 0, beyond < count)
    )
    relays = [flipped(me, far | mask) + edge_side for mask in masks]
    early = far // 2

    def quick(part):
        return functools.reduce(
            jnp.logical_or, [part <= early, part == far - 1, part > far]
        )

    mine, theirs = both(across, quick(me)), both(across, quick(beyond))
    relayed = [
        both(
            to >= 0,
            jnp.logical_or(
                both(high, jnp.logical_or(top, bottom), to <= early), both(low, bottom)
            ),
        )
        for to in relays
    ]
    carrier = both(bottom, me > 0, me <= far)
    carries = [flipped(me - carrier.astype(jnp.int32), far | mask) + 1 for mask in masks]
    carried = [both(carrier, to < count) for to in carries]
    served = both(bottom, me > far)

    loads = [
        pltpu.make_async_copy(src, dst, in_sem.at[i])
        for i, (src, dst) in enumerate(
            [
                (lists_hbm, lists_in), (pos_hbm, pos_in), (vel_hbm, vel_in), (mass_hbm, mass_in),
                (rim_hbm, rim_in), (pair_hbm, pair_in), (tiles_hbm, tiles_in),
            ]
        )
    ]
    for load in loads:
        load.start()

    barrier = pltpu.get_barrier_semaphore()

    def greet(peer):
        pl.semaphore_signal(barrier, inc=1, device_id=(peer,), device_id_type=MESH)

    @pl.when(low)
    def _():
        for mask in masks:
            greet(flipped(me, far | mask))

    for mask in (near, mid):
        greet(flipped(me, mask))
    pl.when(low)(lambda: greet(flipped(me, masks[3])))
    awaited = 3 + 3 * high.astype(jnp.int32)
    lower, upper = both(bottom, across), both(top, across)
    for by, skipped, excused in ((1, upper, False), (-1, False, lower)):
        pl.when(both(inside(by), jnp.logical_not(skipped)))(
            functools.partial(greet, shifted(me, by))
        )
        awaited += both(inside(by), jnp.logical_not(excused)).astype(jnp.int32)
    hailing = both(upper, beyond >= far)
    awaited += 4 * hailing.astype(jnp.int32)
    hailed = [jnp.logical_and(jnp.logical_and(low, bottom), condition) for condition in relayed]
    for to, condition in zip(relays + carries, hailed + carried):
        pl.when(condition)(functools.partial(greet, to))
    awaited += 4 * served.astype(jnp.int32)

    @pl.when(both(across, me <= early))
    def _():
        for mask in masks:
            greet(flipped(beyond, far | mask))

    for condition in relayed:
        awaited += jnp.logical_and(high, condition).astype(jnp.int32)

    routes = [(send_a, recv_a.at[k], flipped(me, far | masks[k]), None, None) for k in range(4)]
    routes += [
        (src, dst.at[k - 1], flipped(me, masks[k]), None, None)
        for src, dst in ((lists_in, recv_l), (send_k, recv_k))
        for k in (1, 2, 3)
    ]
    routes += [
        (src, dst, shifted(me, by), inside(by), inside(-by))
        for src, dst, by in (
            (send_r, recv_r.at[0], 1),
            (send_r, recv_r.at[1], -1),
            (send_c.at[0], recv_c.at[0], 1),
            (send_c.at[1], recv_c.at[1], -1),
            (send_c.at[0], recv_c.at[2], 2),
            (send_c.at[1], recv_c.at[3], -2),
            (send_f.at[0], recv_f.at[0], 1),
            (send_f.at[1], recv_f.at[1], -1),
        )
    ]
    for i, out_gate, in_gate in ((10, top, bottom), (11, bottom, top)):
        routes[i] = routes[i][:3] + tuple(
            both(condition, jnp.logical_not(both(gate, hurried)))
            for condition, gate, hurried in zip(
                routes[i][3:], (out_gate, in_gate), (theirs, mine)
            )
        )
    direct = both(mine, jnp.logical_not(served))
    routes += [(send_a, recv_x.at[k], relays[k], relayed[k], direct) for k in range(4)]
    routes += [(send_e, recv_e, beyond, theirs, mine)]
    routes += [(send_a, recv_p, beyond, both(top, low), carrier)]
    routes += [(recv_p, recv_x.at[k], carries[k], carried[k], served) for k in range(4)]
    copies = [
        pltpu.make_async_remote_copy(
            src_ref=src, dst_ref=dst, send_sem=send_sem.at[i], recv_sem=recv_sem.at[i],
            device_id=(target,), device_id_type=MESH,
        )
        for i, (src, dst, target, _, _) in enumerate(routes)
    ]

    def guarded(action, condition):
        if condition is None:
            action()
        else:
            pl.when(condition)(action)

    def send(*which):
        for i in which:
            guarded(copies[i].start, routes[i][3])

    def receive(*which):
        for i in which:
            guarded(copies[i].wait_recv, routes[i][4])

    def blank(*refs):
        for ref in refs:
            ref[...] = jnp.zeros(ref.shape, F32)

    for load in loads[:4]:
        load.wait()
    put_one_hot(tab0.at[0], lists_in[0:1, :])
    state = rows8(pos_in[...], vel_in[...], mass_in[...])
    send_a[...] = pick(state, tab0[0])

    pl.semaphore_wait(barrier, awaited)

    def tell(semaphore, peer):
        pl.semaphore_signal(semaphore, inc=1, device_id=(peer,), device_id_type=MESH)

    @pl.when(high)
    def _():
        for k in range(4):
            tell(far_sem.at[k], routes[k][2])
        tell(near_sem, flipped(me, near))
        send(18, 19, 20, 21, 0, 1, 2, 3)

    pl.when(upper)(lambda: tell(seen_sem, beyond))

    send(23)

    @pl.when(hailing)
    def _():
        for k in range(4):
            tell(edge_sem.at[k], flipped(beyond, far | masks[k]))

    @pl.when(served)
    def _():
        for k in range(4):
            tell(hail_sem.at[k], flipped(me - 1, far | masks[k]) + 1)

    send(4, 5)
    pl.when(low)(lambda: send(6))
    ones = jnp.ones((8, half), F32)

    def keep(table):
        return 1.0 - spread(ones, table)[:1]

    kept = state * keep(tab0[0])
    send_k[...] = kept
    send(7, 8)
    pl.when(low)(lambda: send(9))

    @pl.when(high)
    def _():
        pl.semaphore_wait(near_sem, 1)
        send(6, 9)

    pl.when(me < 1)(lambda: blank(recv_r.at[0], recv_c.at[0], recv_f.at[0]))
    pl.when(me > count - 2)(lambda: blank(recv_r.at[1], recv_c.at[1], recv_f.at[1]))
    pl.when(me < 2)(lambda: blank(recv_c.at[2]))
    pl.when(me > count - 3)(lambda: blank(recv_c.at[3]))

    loads[4].wait()
    loads[5].wait()
    rim_row = rim_in[...]
    put_one_hot(tab1.at[0], lists_in[1:2, :])
    put_one_hot(tab2.at[0], lists_in[2:3, :])
    put_one_hot(rim_tab, rim_row)
    first, second = pair_in[0:1, :], pair_in[1:2, :]

    def touch(slot):
        return (jnp.where(slot == first, 1.0, 0.0) - jnp.where(slot == second, 1.0, 0.0)).astype(
            BF16
        )

    def put_ends(i, carry):
        slot = lax.broadcasted_iota(jnp.int32, (32, contacts), 0) + i * 32
        ends[pl.ds(pl.multiple_of(i * 32, 32), 32), :] = touch(slot)
        return carry

    extent = grains + 2 * width
    lax.fori_loop(0, extent // 32, put_ends, 0)
    square = lax.broadcasted_iota(jnp.int32, (width, width), 0) == lax.broadcasted_iota(
        jnp.int32, (width, width), 1
    )
    rim_column = jnp.sum(jnp.where(square, rim_row, 0), axis=1, keepdims=True)
    for i in range(0, width, 32):
        ends[extent + i : extent + i + 32, :] = touch(rim_column[i : i + 32])

    loads[6].wait()
    eye = lax.broadcasted_iota(jnp.int32, (tile, tile), 0) == lax.broadcasted_iota(
        jnp.int32, (tile, tile), 1
    )
    diags = []
    for t in range(tiles):
        block = tiles_in[t]
        head = block.astype(BF16)
        tiles_hi[t * tile : (t + 1) * tile, :] = head
        tiles_lo[t * tile : (t + 1) * tile, :] = (block - head.astype(F32)).astype(BF16)
        diags.append(jnp.sum(jnp.where(eye, block, 0.0), axis=0, keepdims=True))
    diag = jnp.concatenate(diags, axis=1)
    own_tile = lax.broadcasted_iota(jnp.int32, (tiles, contacts), 0) == (
        lax.broadcasted_iota(jnp.int32, (tiles, contacts), 1) // tile
    )

    def coupled(lam):
        table = jnp.concatenate(
            [lam[:, t * tile : (t + 1) * tile] for t in range(tiles)], axis=0
        )
        product = spread(table, tiles_hi[...]) + spread(table, tiles_lo[...])
        return jnp.sum(jnp.where(own_tile, product, 0.0), axis=0, keepdims=True)

    lam = jnp.zeros((1, contacts), F32)
    pull = coupled(lam)

    code_row = lax.broadcasted_iota(jnp.int32, (8, half), 0)
    order = lax.broadcasted_iota(jnp.int32, (8, half), 1).astype(F32) + 1.0

    def coded(k, rows):
        codes = spread(jnp.where(code_row == k, order, 0.0), tab0[k])
        return jnp.concatenate([rows, codes], axis=0)

    def answer():
        for k in range(4):
            pl.semaphore_wait(far_sem.at[k], 1)
            send(k)

    def carry():
        receive(23)
        for k in range(4):

            @pl.when(carried[k])
            def _():
                pl.semaphore_wait(hail_sem.at[k], 1)
                copies[24 + k].start()

    pl.when(both(low, me >= early))(answer)
    pl.when(both(carrier, me >= early))(carry)
    parts = [coded(0, kept)]
    for k in (1, 2, 3):
        receive(3 + k)
        put_one_hot(tab0.at[k], recv_l[k - 1, 0:1, :])
        put_one_hot(tab1.at[k], recv_l[k - 1, 1:2, :])
        if k == 1:
            put_one_hot(tab2.at[1], recv_l[0, 2:3, :])
        receive(6 + k)
        parts.append(coded(k, recv_k[k - 1]))
    pair = [
        parts[k] * keep(tab1[k]) + spread(pick(parts[k + 2], tab1[k + 2]), tab1[k])
        for k in (0, 1)
    ]
    state = pair[0] * keep(tab2[0]) + spread(pick(pair[1], tab2[1]), tab2[0])
    edge = pick(state, rim_tab[...])
    send_e[...] = edge
    pl.when(lower)(lambda: pl.semaphore_wait(seen_sem, 1))
    send(22)
    for k in range(4):
        put_one_hot(
            edge_tab.at[k * half : (k + 1) * half, :], edge[8 + k : 9 + k].astype(jnp.int32), 1
        )
        put_one_hot(
            slot_tab.at[k * half : (k + 1) * half, :], state[8 + k : 9 + k].astype(jnp.int32), 1
        )

    pl.when(me < early)(answer)
    pl.when(both(carrier, me < early))(carry)
    for k in range(4):

        @pl.when(hailed[k])
        def _():
            pl.semaphore_wait(edge_sem.at[k], 1)
            copies[18 + k].start()

    receive(2, 3, 1, 0)
    arrived = split(jnp.concatenate([recv_a[k] for k in range(4)], axis=1))
    edge = edge[:8] + join(jnp.dot(arrived, edge_tab[...], preferred_element_type=F32))
    send_r[...] = edge
    send(10, 11)
    state = state[:8] + join(jnp.dot(arrived, slot_tab[...], preferred_element_type=F32))
    vel, mass = state[3:6], state[6:7]
    gathered = pick(state, ends[:grains, :])

    @pl.when(mine)
    def _():
        receive(22)
        for k in range(4):
            put_one_hot(
                cross_tab.at[k * half : (k + 1) * half, :],
                recv_e[8 + k : 9 + k, :].astype(jnp.int32), 1,
            )
        receive(20, 21, 19, 18, 26, 27, 25, 24)
        seen = split(jnp.concatenate([recv_x[k] for k in range(4)], axis=1))
        recv_r[top.astype(jnp.int32)] = recv_e[:8] + join(
            jnp.dot(seen, cross_tab[...], preferred_element_type=F32)
        )

    receive(10, 11)
    left, right = recv_r[0], recv_r[1]
    gathered += pick(jnp.concatenate([left, right], axis=1), ends[grains:extent, :])
    normal = gathered[0:3]
    speed = jnp.sum(normal * gathered[3:6], axis=0, keepdims=True)
    lam = jnp.maximum(0.0, lam - (pull + speed) / diag)
    force = rows8(normal * lam)
    partial = spread(force, ends[grains:, :])[0:3]
    ghost_left, ghost_right = partial[:, :width], partial[:, width : 2 * width]
    at_rim = partial[:, 2 * width :]
    send_c[0] = rows8(ghost_right, at_rim)
    send_c[1] = rows8(ghost_left, at_rim)
    send(12, 13, 14, 15)
    local = spread(force, ends[:grains, :])[0:3]
    base = pick(rows8(vel + mass * local), ends[:grains, :])[0:3]
    pull = coupled(lam)

    receive(12, 13, 14, 15)
    incoming = edge[6:7] * (recv_c[0, 0:3] + recv_c[1, 0:3])
    fresh_left = left[3:6] + left[6:7] * (recv_c[0, 3:6] + ghost_left + recv_c[2, 0:3])
    fresh_right = right[3:6] + right[6:7] * (recv_c[1, 3:6] + ghost_right + recv_c[3, 0:3])
    relative = base + pick(
        rows8(jnp.concatenate([fresh_left, fresh_right, incoming], axis=1)), ends[grains:, :]
    )[0:3]
    speed = jnp.sum(normal * relative, axis=0, keepdims=True)
    lam = jnp.maximum(0.0, lam - (pull + speed) / diag)
    force = rows8(normal * lam)
    partial = spread(force, ends[grains:extent, :])
    send_f[0] = partial[:, width:]
    send_f[1] = partial[:, :width]
    send(16, 17)
    lam_out[...] = lam
    base = vel + mass * spread(force, ends[:grains, :])[0:3]

    receive(16, 17)
    vel_out[...] = base + mass * spread(recv_f[0] + recv_f[1], rim_tab[...])[0:3]
    for i in range(MESSAGES):
        guarded(copies[i].wait_send, routes[i][3])


def body(count, positions, velocity, inv_mass, swap_lists, rim_list, contact_pair, delassus):
    grains = positions.shape[1]
    half = swap_lists.shape[1]
    width = rim_list.shape[0]
    contacts = contact_pair.shape[1]
    tiles, tile = delassus.shape[:2]
    args = (
        positions, velocity, inv_mass.reshape(1, grains), swap_lists, rim_list.reshape(1, width),
        contact_pair, delassus,
    )
    args = tuple(pltpu.with_memory_space_constraint(arg, pltpu.HBM) for arg in args)

    current, lam = pl.pallas_call(
        lambda *refs: kernel(count, *refs),
        out_shape=(
            jax.ShapeDtypeStruct((3, grains), F32),
            jax.ShapeDtypeStruct((1, contacts), F32),
        ),
        in_specs=[pl.BlockSpec(memory_space=pltpu.HBM)] * len(args),
        out_specs=(
            pl.BlockSpec(memory_space=pltpu.VMEM),
            pl.BlockSpec(memory_space=pltpu.VMEM),
        ),
        scratch_shapes=[pltpu.VMEM(arg.shape, arg.dtype) for arg in args]
        + [
            pltpu.VMEM((grains + 3 * width, contacts), BF16),
            pltpu.VMEM((4, grains, half), BF16),
            pltpu.VMEM((4, grains, half), BF16),
            pltpu.VMEM((2, grains, half), BF16),
            pltpu.VMEM((grains, width), BF16),
            pltpu.VMEM((4 * half, grains), BF16),
            pltpu.VMEM((4 * half, width), BF16),
            pltpu.VMEM((4 * half, width), BF16),
            pltpu.VMEM((contacts, tile), BF16),
            pltpu.VMEM((contacts, tile), BF16),
            pltpu.VMEM((8, half), F32),
            pltpu.VMEM((8, grains), F32),
            pltpu.VMEM((8, width), F32),
            pltpu.VMEM((2, 8, width), F32),
            pltpu.VMEM((2, 8, width), F32),
            pltpu.VMEM((16, width), F32),
            pltpu.VMEM((4, 8, half), F32),
            pltpu.VMEM((3, 3, half), jnp.int32),
            pltpu.VMEM((3, 8, grains), F32),
            pltpu.VMEM((2, 8, width), F32),
            pltpu.VMEM((4, 8, width), F32),
            pltpu.VMEM((2, 8, width), F32),
            pltpu.VMEM((4, 8, half), F32),
            pltpu.VMEM((16, width), F32),
            pltpu.VMEM((8, half), F32),
            pltpu.SemaphoreType.DMA((len(args),)),
            pltpu.SemaphoreType.DMA((MESSAGES,)),
            pltpu.SemaphoreType.DMA((MESSAGES,)),
            pltpu.SemaphoreType.REGULAR((4,)),
            pltpu.SemaphoreType.REGULAR((4,)),
            pltpu.SemaphoreType.REGULAR((4,)),
            pltpu.SemaphoreType.REGULAR,
            pltpu.SemaphoreType.REGULAR,
        ],
        compiler_params=pltpu.CompilerParams(
            collective_id=0, has_side_effects=True, vmem_limit_bytes=32 << 20
        ),
        name="contact_step",
    )(*args)
    return current, lam.reshape(contacts)


def solution(mesh):
    count = mesh.shape["parts"]
    in_specs = (
        P(None, "parts"),
        P(None, "parts"),
        P("parts"),
        P(None, "parts"),
        P("parts"),
        P(None, "parts"),
        P("parts", None, None),
    )
    out_specs = (P(None, "parts"), P("parts"))
    return jax.shard_map(
        lambda *args: body(count, *args),
        mesh=mesh, in_specs=in_specs, out_specs=out_specs, check_vma=False,
    )
```

```python
import functools

import jax
import jax.numpy as jnp
from jax import lax
from jax.experimental import pallas as pl
from jax.experimental.pallas import tpu as pltpu
from jax.sharding import PartitionSpec as P

MESH = pl.DeviceIdType.MESH
F32 = jnp.float32
BF16 = jnp.bfloat16
MESSAGES = 28


def split(x):
    head = x.astype(BF16).astype(F32)
    return jnp.concatenate([head, x - head], axis=0).astype(BF16)


def join(y):
    half = y.shape[0] // 2
    return y[:half] + y[half:]


def pick(x, table):
    return join(jnp.dot(split(x), table, preferred_element_type=F32))


def spread(x, table):
    return join(
        lax.dot_general(split(x), table, (((1,), (1,)), ((), ())), preferred_element_type=F32)
    )


def rows8(*pieces):
    have = sum(piece.shape[0] for piece in pieces)
    if have < 8:
        pieces += (jnp.zeros((8 - have, pieces[0].shape[1]), F32),)
    return jnp.concatenate(pieces, axis=0)


def put_one_hot(table, row, base=0):
    extent, width = table.shape
    block = 64

    def step(i, carry):
        slot = lax.broadcasted_iota(jnp.int32, (block, width), 0) + (i * block + base)
        table[pl.ds(pl.multiple_of(i * block, block), block), :] = jnp.where(
            slot == row, 1.0, 0.0
        ).astype(BF16)
        return carry

    lax.fori_loop(0, extent // block, step, 0)


def kernel(
    count,
    pos_hbm, vel_hbm, mass_hbm, lists_hbm, rim_hbm, pair_hbm, tiles_hbm,
    vel_out, lam_out,
    pos_in, vel_in, mass_in, lists_in, rim_in, pair_in, tiles_in,
    ends, tab0, tab1, tab2, rim_tab, slot_tab, edge_tab, cross_tab, tiles_hi, tiles_lo,
    send_a, send_k, send_r, send_c, send_f, send_e,
    recv_a, recv_l, recv_k, recv_r, recv_c, recv_f, recv_x, recv_e, recv_p,
    in_sem, send_sem, recv_sem, far_sem, edge_sem, hail_sem, near_sem, seen_sem,
):
    grains = pos_in.shape[1]
    half = lists_in.shape[1]
    width = rim_in.shape[1]
    contacts = pair_in.shape[1]
    tiles, tile = tiles_in.shape[:2]
    bits = count.bit_length() - 1
    far, mid, near = (1 << (bits - 1 - level) for level in range(3))
    masks = (0, near, mid, mid | near)
    plane = count // 16
    me = lax.axis_index("parts")
    high = me >= far
    low = me < far

    def shifted(base, by):
        return lax.rem(base + (by + count), count)

    def flipped(base, mask):
        return lax.bitwise_xor(base, jnp.int32(mask))

    def both(*conditions):
        return functools.reduce(jnp.logical_and, conditions)

    def inside(by):
        return me >= -by if by < 0 else me < count - by

    spot = lax.rem(me, plane)
    top, bottom = spot == plane - 1, spot == 0
    edge_side = jnp.where(top, 1, -1)
    beyond = me + edge_side
    across = jnp.logical_and(
        jnp.logical_or(top, bottom), jnp.logical_and(beyond >= 0, beyond < count)
    )
    relays = [flipped(me, far | mask) + edge_side for mask in masks]
    early = far // 2

    def quick(part):
        return functools.reduce(
            jnp.logical_or, [part <= early, part == far - 1, part > far, part == early + plane]
        )

    mine, theirs = both(across, quick(me)), both(across, quick(beyond))
    relayed = [
        both(
            to >= 0,
            jnp.logical_or(
                both(high, jnp.logical_or(top, bottom), to < far - 1, quick(to)),
                both(low, bottom),
            ),
        )
        for to in relays
    ]
    carrier = both(bottom, me > 0, me <= far)
    carries = [flipped(me - carrier.astype(jnp.int32), far | mask) + 1 for mask in masks]
    carried = [both(carrier, to < count) for to in carries]
    served = both(bottom, me > far)

    loads = [
        pltpu.make_async_copy(src, dst, in_sem.at[i])
        for i, (src, dst) in enumerate(
            [
                (lists_hbm, lists_in), (pos_hbm, pos_in), (vel_hbm, vel_in), (mass_hbm, mass_in),
                (rim_hbm, rim_in), (pair_hbm, pair_in), (tiles_hbm, tiles_in),
            ]
        )
    ]
    for load in loads:
        load.start()

    barrier = pltpu.get_barrier_semaphore()

    def greet(peer):
        pl.semaphore_signal(barrier, inc=1, device_id=(peer,), device_id_type=MESH)

    @pl.when(low)
    def _():
        for mask in masks:
            greet(flipped(me, far | mask))

    for mask in (near, mid):
        greet(flipped(me, mask))
    pl.when(low)(lambda: greet(flipped(me, masks[3])))
    awaited = 3 + 3 * high.astype(jnp.int32)
    lower, upper = both(bottom, across), both(top, across)
    for by, skipped, excused in ((1, upper, False), (-1, False, lower)):
        pl.when(both(inside(by), jnp.logical_not(skipped)))(
            functools.partial(greet, shifted(me, by))
        )
        awaited += both(inside(by), jnp.logical_not(excused)).astype(jnp.int32)
    hailing = both(upper, beyond >= far)
    awaited += 4 * hailing.astype(jnp.int32)
    hailed = [jnp.logical_and(jnp.logical_and(low, bottom), condition) for condition in relayed]
    for to, condition in zip(relays + carries, hailed + carried):
        pl.when(condition)(functools.partial(greet, to))
    awaited += 4 * served.astype(jnp.int32)

    @pl.when(both(mine, me < far - 1))
    def _():
        for mask in masks:
            greet(flipped(beyond, far | mask))

    for condition in relayed:
        awaited += jnp.logical_and(high, condition).astype(jnp.int32)

    routes = [(send_a, recv_a.at[k], flipped(me, far | masks[k]), None, None) for k in range(4)]
    routes += [
        (src, dst.at[k - 1], flipped(me, masks[k]), None, None)
        for src, dst in ((lists_in, recv_l), (send_k, recv_k))
        for k in (1, 2, 3)
    ]
    routes += [
        (src, dst, shifted(me, by), inside(by), inside(-by))
        for src, dst, by in (
            (send_r, recv_r.at[0], 1),
            (send_r, recv_r.at[1], -1),
            (send_c.at[0], recv_c.at[0], 1),
            (send_c.at[1], recv_c.at[1], -1),
            (send_c.at[0], recv_c.at[2], 2),
            (send_c.at[1], recv_c.at[3], -2),
            (send_f.at[0], recv_f.at[0], 1),
            (send_f.at[1], recv_f.at[1], -1),
        )
    ]
    for i, out_gate, in_gate in ((10, top, bottom), (11, bottom, top)):
        routes[i] = routes[i][:3] + tuple(
            both(condition, jnp.logical_not(both(gate, hurried)))
            for condition, gate, hurried in zip(
                routes[i][3:], (out_gate, in_gate), (theirs, mine)
            )
        )
    direct = both(mine, jnp.logical_not(served))
    routes += [(send_a, recv_x.at[k], relays[k], relayed[k], direct) for k in range(4)]
    routes += [(send_e, recv_e, beyond, theirs, mine)]
    routes += [(send_a, recv_p, beyond, both(top, low), carrier)]
    routes += [(recv_p, recv_x.at[k], carries[k], carried[k], served) for k in range(4)]
    copies = [
        pltpu.make_async_remote_copy(
            src_ref=src, dst_ref=dst, send_sem=send_sem.at[i], recv_sem=recv_sem.at[i],
            device_id=(target,), device_id_type=MESH,
        )
        for i, (src, dst, target, _, _) in enumerate(routes)
    ]

    def guarded(action, condition):
        if condition is None:
            action()
        else:
            pl.when(condition)(action)

    def send(*which):
        for i in which:
            guarded(copies[i].start, routes[i][3])

    def receive(*which):
        for i in which:
            guarded(copies[i].wait_recv, routes[i][4])

    def blank(*refs):
        for ref in refs:
            ref[...] = jnp.zeros(ref.shape, F32)

    for load in loads[:4]:
        load.wait()
    put_one_hot(tab0.at[0], lists_in[0:1, :])
    state = rows8(pos_in[...], vel_in[...], mass_in[...])
    send_a[...] = pick(state, tab0[0])

    pl.semaphore_wait(barrier, awaited)

    def tell(semaphore, peer):
        pl.semaphore_signal(semaphore, inc=1, device_id=(peer,), device_id_type=MESH)

    @pl.when(high)
    def _():
        send(18, 19, 20, 21)
        for k in range(4):
            tell(far_sem.at[k], routes[k][2])
        send(0, 1, 2, 3)
        tell(near_sem, flipped(me, near))

    pl.when(upper)(lambda: tell(seen_sem, beyond))

    send(23)

    @pl.when(hailing)
    def _():
        for k in range(4):
            tell(edge_sem.at[k], flipped(beyond, far | masks[k]))

    @pl.when(served)
    def _():
        for k in range(4):
            tell(hail_sem.at[k], flipped(me - 1, far | masks[k]) + 1)

    send(4, 5)
    pl.when(low)(lambda: send(6))
    ones = jnp.ones((8, half), F32)

    def keep(table):
        return 1.0 - spread(ones, table)[:1]

    kept = state * keep(tab0[0])
    send_k[...] = kept
    send(7, 8)
    pl.when(low)(lambda: send(9))

    @pl.when(high)
    def _():
        pl.semaphore_wait(near_sem, 1)
        send(6, 9)

    pl.when(me < 1)(lambda: blank(recv_r.at[0], recv_c.at[0], recv_f.at[0]))
    pl.when(me > count - 2)(lambda: blank(recv_r.at[1], recv_c.at[1], recv_f.at[1]))
    pl.when(me < 2)(lambda: blank(recv_c.at[2]))
    pl.when(me > count - 3)(lambda: blank(recv_c.at[3]))

    loads[4].wait()
    loads[5].wait()
    rim_row = rim_in[...]
    put_one_hot(tab1.at[0], lists_in[1:2, :])
    put_one_hot(tab2.at[0], lists_in[2:3, :])
    put_one_hot(rim_tab, rim_row)
    first, second = pair_in[0:1, :], pair_in[1:2, :]

    def touch(slot):
        return (jnp.where(slot == first, 1.0, 0.0) - jnp.where(slot == second, 1.0, 0.0)).astype(
            BF16
        )

    def put_ends(i, carry):
        slot = lax.broadcasted_iota(jnp.int32, (32, contacts), 0) + i * 32
        ends[pl.ds(pl.multiple_of(i * 32, 32), 32), :] = touch(slot)
        return carry

    extent = grains + 2 * width
    lax.fori_loop(0, extent // 32, put_ends, 0)
    square = lax.broadcasted_iota(jnp.int32, (width, width), 0) == lax.broadcasted_iota(
        jnp.int32, (width, width), 1
    )
    rim_column = jnp.sum(jnp.where(square, rim_row, 0), axis=1, keepdims=True)
    for i in range(0, width, 32):
        ends[extent + i : extent + i + 32, :] = touch(rim_column[i : i + 32])

    loads[6].wait()
    eye = lax.broadcasted_iota(jnp.int32, (tile, tile), 0) == lax.broadcasted_iota(
        jnp.int32, (tile, tile), 1
    )
    diags = []
    for t in range(tiles):
        block = tiles_in[t]
        head = block.astype(BF16)
        tiles_hi[t * tile : (t + 1) * tile, :] = head
        tiles_lo[t * tile : (t + 1) * tile, :] = (block - head.astype(F32)).astype(BF16)
        diags.append(jnp.sum(jnp.where(eye, block, 0.0), axis=0, keepdims=True))
    diag = jnp.concatenate(diags, axis=1)
    own_tile = lax.broadcasted_iota(jnp.int32, (tiles, contacts), 0) == (
        lax.broadcasted_iota(jnp.int32, (tiles, contacts), 1) // tile
    )

    def coupled(lam):
        table = jnp.concatenate(
            [lam[:, t * tile : (t + 1) * tile] for t in range(tiles)], axis=0
        )
        product = spread(table, tiles_hi[...]) + spread(table, tiles_lo[...])
        return jnp.sum(jnp.where(own_tile, product, 0.0), axis=0, keepdims=True)

    lam = jnp.zeros((1, contacts), F32)
    pull = coupled(lam)

    code_row = lax.broadcasted_iota(jnp.int32, (8, half), 0)
    order = lax.broadcasted_iota(jnp.int32, (8, half), 1).astype(F32) + 1.0

    def coded(k, rows):
        codes = spread(jnp.where(code_row == k, order, 0.0), tab0[k])
        return jnp.concatenate([rows, codes], axis=0)

    def answer():
        for k in range(4):
            pl.semaphore_wait(far_sem.at[k], 1)
            send(k)

    def carry():
        receive(23)
        for k in range(4):

            @pl.when(carried[k])
            def _():
                pl.semaphore_wait(hail_sem.at[k], 1)
                copies[24 + k].start()

    pl.when(both(low, me >= early))(answer)
    pl.when(both(carrier, me >= early))(carry)
    parts = [coded(0, kept)]
    for k in (1, 2, 3):
        receive(3 + k)
        put_one_hot(tab0.at[k], recv_l[k - 1, 0:1, :])
        put_one_hot(tab1.at[k], recv_l[k - 1, 1:2, :])
        if k == 1:
            put_one_hot(tab2.at[1], recv_l[0, 2:3, :])
        receive(6 + k)
        parts.append(coded(k, recv_k[k - 1]))
    pair = [
        parts[k] * keep(tab1[k]) + spread(pick(parts[k + 2], tab1[k + 2]), tab1[k])
        for k in (0, 1)
    ]
    state = pair[0] * keep(tab2[0]) + spread(pick(pair[1], tab2[1]), tab2[0])
    edge = pick(state, rim_tab[...])
    send_e[...] = edge
    pl.when(lower)(lambda: pl.semaphore_wait(seen_sem, 1))
    send(22)
    for k in range(4):
        put_one_hot(
            edge_tab.at[k * half : (k + 1) * half, :], edge[8 + k : 9 + k].astype(jnp.int32), 1
        )
        put_one_hot(
            slot_tab.at[k * half : (k + 1) * half, :], state[8 + k : 9 + k].astype(jnp.int32), 1
        )

    pl.when(me < early)(answer)
    pl.when(both(carrier, me < early))(carry)
    for k in range(4):

        @pl.when(hailed[k])
        def _():
            pl.semaphore_wait(edge_sem.at[k], 1)
            copies[18 + k].start()

    receive(2, 3, 1, 0)
    arrived = split(jnp.concatenate([recv_a[k] for k in range(4)], axis=1))
    edge = edge[:8] + join(jnp.dot(arrived, edge_tab[...], preferred_element_type=F32))
    send_r[...] = edge
    send(10, 11)
    state = state[:8] + join(jnp.dot(arrived, slot_tab[...], preferred_element_type=F32))
    vel, mass = state[3:6], state[6:7]
    gathered = pick(state, ends[:grains, :])

    @pl.when(mine)
    def _():
        receive(22)
        for k in range(4):
            put_one_hot(
                cross_tab.at[k * half : (k + 1) * half, :],
                recv_e[8 + k : 9 + k, :].astype(jnp.int32), 1,
            )
        receive(20, 21, 19, 18, 26, 27, 25, 24)
        seen = split(jnp.concatenate([recv_x[k] for k in range(4)], axis=1))
        recv_r[top.astype(jnp.int32)] = recv_e[:8] + join(
            jnp.dot(seen, cross_tab[...], preferred_element_type=F32)
        )

    receive(10, 11)
    left, right = recv_r[0], recv_r[1]
    gathered += pick(jnp.concatenate([left, right], axis=1), ends[grains:extent, :])
    normal = gathered[0:3]
    speed = jnp.sum(normal * gathered[3:6], axis=0, keepdims=True)
    lam = jnp.maximum(0.0, lam - (pull + speed) / diag)
    force = rows8(normal * lam)
    partial = spread(force, ends[grains:, :])[0:3]
    ghost_left, ghost_right = partial[:, :width], partial[:, width : 2 * width]
    at_rim = partial[:, 2 * width :]
    send_c[0] = rows8(ghost_right, at_rim)
    send_c[1] = rows8(ghost_left, at_rim)
    send(12, 13, 14, 15)
    local = spread(force, ends[:grains, :])[0:3]
    base = pick(rows8(vel + mass * local), ends[:grains, :])[0:3]
    pull = coupled(lam)

    receive(12, 13, 14, 15)
    incoming = edge[6:7] * (recv_c[0, 0:3] + recv_c[1, 0:3])
    fresh_left = left[3:6] + left[6:7] * (recv_c[0, 3:6] + ghost_left + recv_c[2, 0:3])
    fresh_right = right[3:6] + right[6:7] * (recv_c[1, 3:6] + ghost_right + recv_c[3, 0:3])
    relative = base + pick(
        rows8(jnp.concatenate([fresh_left, fresh_right, incoming], axis=1)), ends[grains:, :]
    )[0:3]
    speed = jnp.sum(normal * relative, axis=0, keepdims=True)
    lam = jnp.maximum(0.0, lam - (pull + speed) / diag)
    force = rows8(normal * lam)
    partial = spread(force, ends[grains:extent, :])
    send_f[0] = partial[:, width:]
    send_f[1] = partial[:, :width]
    send(16, 17)
    lam_out[...] = lam
    base = vel + mass * spread(force, ends[:grains, :])[0:3]

    receive(16, 17)
    vel_out[...] = base + mass * spread(recv_f[0] + recv_f[1], rim_tab[...])[0:3]
    for i in range(MESSAGES):
        guarded(copies[i].wait_send, routes[i][3])


def body(count, positions, velocity, inv_mass, swap_lists, rim_list, contact_pair, delassus):
    grains = positions.shape[1]
    half = swap_lists.shape[1]
    width = rim_list.shape[0]
    contacts = contact_pair.shape[1]
    tiles, tile = delassus.shape[:2]
    args = (
        positions, velocity, inv_mass.reshape(1, grains), swap_lists, rim_list.reshape(1, width),
        contact_pair, delassus,
    )
    args = tuple(pltpu.with_memory_space_constraint(arg, pltpu.HBM) for arg in args)

    current, lam = pl.pallas_call(
        lambda *refs: kernel(count, *refs),
        out_shape=(
            jax.ShapeDtypeStruct((3, grains), F32),
            jax.ShapeDtypeStruct((1, contacts), F32),
        ),
        in_specs=[pl.BlockSpec(memory_space=pltpu.HBM)] * len(args),
        out_specs=(
            pl.BlockSpec(memory_space=pltpu.VMEM),
            pl.BlockSpec(memory_space=pltpu.VMEM),
        ),
        scratch_shapes=[pltpu.VMEM(arg.shape, arg.dtype) for arg in args]
        + [
            pltpu.VMEM((grains + 3 * width, contacts), BF16),
            pltpu.VMEM((4, grains, half), BF16),
            pltpu.VMEM((4, grains, half), BF16),
            pltpu.VMEM((2, grains, half), BF16),
            pltpu.VMEM((grains, width), BF16),
            pltpu.VMEM((4 * half, grains), BF16),
            pltpu.VMEM((4 * half, width), BF16),
            pltpu.VMEM((4 * half, width), BF16),
            pltpu.VMEM((contacts, tile), BF16),
            pltpu.VMEM((contacts, tile), BF16),
            pltpu.VMEM((8, half), F32),
            pltpu.VMEM((8, grains), F32),
            pltpu.VMEM((8, width), F32),
            pltpu.VMEM((2, 8, width), F32),
            pltpu.VMEM((2, 8, width), F32),
            pltpu.VMEM((16, width), F32),
            pltpu.VMEM((4, 8, half), F32),
            pltpu.VMEM((3, 3, half), jnp.int32),
            pltpu.VMEM((3, 8, grains), F32),
            pltpu.VMEM((2, 8, width), F32),
            pltpu.VMEM((4, 8, width), F32),
            pltpu.VMEM((2, 8, width), F32),
            pltpu.VMEM((4, 8, half), F32),
            pltpu.VMEM((16, width), F32),
            pltpu.VMEM((8, half), F32),
            pltpu.SemaphoreType.DMA((len(args),)),
            pltpu.SemaphoreType.DMA((MESSAGES,)),
            pltpu.SemaphoreType.DMA((MESSAGES,)),
            pltpu.SemaphoreType.REGULAR((4,)),
            pltpu.SemaphoreType.REGULAR((4,)),
            pltpu.SemaphoreType.REGULAR((4,)),
            pltpu.SemaphoreType.REGULAR,
            pltpu.SemaphoreType.REGULAR,
        ],
        compiler_params=pltpu.CompilerParams(
            collective_id=0, has_side_effects=True, vmem_limit_bytes=32 << 20
        ),
        name="contact_step",
    )(*args)
    return current, lam.reshape(contacts)


def solution(mesh):
    count = mesh.shape["parts"]
    in_specs = (
        P(None, "parts"),
        P(None, "parts"),
        P("parts"),
        P(None, "parts"),
        P("parts"),
        P(None, "parts"),
        P("parts", None, None),
    )
    out_specs = (P(None, "parts"), P("parts"))
    return jax.shard_map(
        lambda *args: body(count, *args),
        mesh=mesh, in_specs=in_specs, out_specs=out_specs, check_vma=False,
    )
```

```python
import functools

import jax
import jax.numpy as jnp
from jax import lax
from jax.experimental import pallas as pl
from jax.experimental.pallas import tpu as pltpu
from jax.sharding import PartitionSpec as P

MESH = pl.DeviceIdType.MESH
F32 = jnp.float32
BF16 = jnp.bfloat16
MESSAGES = 28


def split(x):
    head = x.astype(BF16).astype(F32)
    return jnp.concatenate([head, x - head], axis=0).astype(BF16)


def join(y):
    half = y.shape[0] // 2
    return y[:half] + y[half:]


def pick(x, table):
    return join(jnp.dot(split(x), table, preferred_element_type=F32))


def spread(x, table):
    return join(
        lax.dot_general(split(x), table, (((1,), (1,)), ((), ())), preferred_element_type=F32)
    )


def rows8(*pieces):
    have = sum(piece.shape[0] for piece in pieces)
    if have < 8:
        pieces += (jnp.zeros((8 - have, pieces[0].shape[1]), F32),)
    return jnp.concatenate(pieces, axis=0)


def put_one_hot(table, row, base=0):
    extent, width = table.shape
    block = 64

    def step(i, carry):
        slot = lax.broadcasted_iota(jnp.int32, (block, width), 0) + (i * block + base)
        table[pl.ds(pl.multiple_of(i * block, block), block), :] = jnp.where(
            slot == row, 1.0, 0.0
        ).astype(BF16)
        return carry

    lax.fori_loop(0, extent // block, step, 0)


def kernel(
    count,
    pos_hbm, vel_hbm, mass_hbm, lists_hbm, rim_hbm, pair_hbm, tiles_hbm,
    vel_out, lam_out,
    pos_in, vel_in, mass_in, lists_in, rim_in, pair_in, tiles_in,
    ends, tab0, tab1, tab2, rim_tab, slot_tab, edge_tab, cross_tab, tiles_hi, tiles_lo,
    send_a, send_k, send_r, send_c, send_f, send_e,
    recv_a, recv_l, recv_k, recv_r, recv_c, recv_f, recv_x, recv_e, recv_p,
    in_sem, send_sem, recv_sem, far_sem, edge_sem, hail_sem, near_sem, seen_sem,
):
    grains = pos_in.shape[1]
    half = lists_in.shape[1]
    width = rim_in.shape[1]
    contacts = pair_in.shape[1]
    tiles, tile = tiles_in.shape[:2]
    bits = count.bit_length() - 1
    far, mid, near = (1 << (bits - 1 - level) for level in range(3))
    masks = (0, near, mid, mid | near)
    plane = count // 16
    me = lax.axis_index("parts")
    high = me >= far
    low = me < far

    def shifted(base, by):
        return lax.rem(base + (by + count), count)

    def flipped(base, mask):
        return lax.bitwise_xor(base, jnp.int32(mask))

    def both(*conditions):
        return functools.reduce(jnp.logical_and, conditions)

    def inside(by):
        return me >= -by if by < 0 else me < count - by

    spot = lax.rem(me, plane)
    top, bottom = spot == plane - 1, spot == 0
    edge_side = jnp.where(top, 1, -1)
    beyond = me + edge_side
    across = jnp.logical_and(
        jnp.logical_or(top, bottom), jnp.logical_and(beyond >= 0, beyond < count)
    )
    relays = [flipped(me, far | mask) + edge_side for mask in masks]
    early = far // 2

    def quick(part):
        return functools.reduce(
            jnp.logical_or, [part <= early, part == far - 1, part > far, part == early + plane]
        )

    mine, theirs = both(across, quick(me)), both(across, quick(beyond))
    relayed = [
        both(
            to >= 0,
            jnp.logical_or(
                both(high, jnp.logical_or(top, bottom), to < far - 1, quick(to)),
                both(low, bottom),
            ),
        )
        for to in relays
    ]
    carrier = both(bottom, me > 0, me <= far)
    carries = [flipped(me - carrier.astype(jnp.int32), far | mask) + 1 for mask in masks]
    carried = [both(carrier, to < count) for to in carries]
    served = both(bottom, me > far)

    loads = [
        pltpu.make_async_copy(src, dst, in_sem.at[i])
        for i, (src, dst) in enumerate(
            [
                (lists_hbm, lists_in), (pos_hbm, pos_in), (vel_hbm, vel_in), (mass_hbm, mass_in),
                (rim_hbm, rim_in), (pair_hbm, pair_in), (tiles_hbm, tiles_in),
            ]
        )
    ]
    for load in loads:
        load.start()

    barrier = pltpu.get_barrier_semaphore()

    def greet(peer):
        pl.semaphore_signal(barrier, inc=1, device_id=(peer,), device_id_type=MESH)

    @pl.when(low)
    def _():
        for mask in masks:
            greet(flipped(me, far | mask))

    for mask in (near, mid):
        greet(flipped(me, mask))
    pl.when(low)(lambda: greet(flipped(me, masks[3])))
    awaited = 3 + 3 * high.astype(jnp.int32)
    lower, upper = both(bottom, across), both(top, across)
    for by, skipped, excused in ((1, upper, False), (-1, False, lower)):
        pl.when(both(inside(by), jnp.logical_not(skipped)))(
            functools.partial(greet, shifted(me, by))
        )
        awaited += both(inside(by), jnp.logical_not(excused)).astype(jnp.int32)
    hailing = both(upper, beyond >= far)
    awaited += 4 * hailing.astype(jnp.int32)
    hailed = [jnp.logical_and(jnp.logical_and(low, bottom), condition) for condition in relayed]
    for to, condition in zip(relays + carries, hailed + carried):
        pl.when(condition)(functools.partial(greet, to))
    awaited += 4 * served.astype(jnp.int32)

    @pl.when(both(mine, me < far - 1))
    def _():
        for mask in masks:
            greet(flipped(beyond, far | mask))

    for condition in relayed:
        awaited += jnp.logical_and(high, condition).astype(jnp.int32)

    routes = [(send_a, recv_a.at[k], flipped(me, far | masks[k]), None, None) for k in range(4)]
    routes += [
        (src, dst.at[k - 1], flipped(me, masks[k]), None, None)
        for src, dst in ((lists_in, recv_l), (send_k, recv_k))
        for k in (1, 2, 3)
    ]
    routes += [
        (src, dst, shifted(me, by), inside(by), inside(-by))
        for src, dst, by in (
            (send_r, recv_r.at[0], 1),
            (send_r, recv_r.at[1], -1),
            (send_c.at[0], recv_c.at[0], 1),
            (send_c.at[1], recv_c.at[1], -1),
            (send_c.at[0], recv_c.at[2], 2),
            (send_c.at[1], recv_c.at[3], -2),
            (send_f.at[0], recv_f.at[0], 1),
            (send_f.at[1], recv_f.at[1], -1),
        )
    ]
    for i, out_gate, in_gate in ((10, top, bottom), (11, bottom, top)):
        routes[i] = routes[i][:3] + tuple(
            both(condition, jnp.logical_not(both(gate, hurried)))
            for condition, gate, hurried in zip(
                routes[i][3:], (out_gate, in_gate), (theirs, mine)
            )
        )
    direct = both(mine, jnp.logical_not(served))
    routes += [(send_a, recv_x.at[k], relays[k], relayed[k], direct) for k in range(4)]
    routes += [(send_e, recv_e, beyond, theirs, mine)]
    routes += [(send_a, recv_p, beyond, both(top, low), carrier)]
    routes += [(recv_p, recv_x.at[k], carries[k], carried[k], served) for k in range(4)]
    copies = [
        pltpu.make_async_remote_copy(
            src_ref=src, dst_ref=dst, send_sem=send_sem.at[i], recv_sem=recv_sem.at[i],
            device_id=(target,), device_id_type=MESH,
        )
        for i, (src, dst, target, _, _) in enumerate(routes)
    ]

    def guarded(action, condition):
        if condition is None:
            action()
        else:
            pl.when(condition)(action)

    def send(*which):
        for i in which:
            guarded(copies[i].start, routes[i][3])

    def receive(*which):
        for i in which:
            guarded(copies[i].wait_recv, routes[i][4])

    def blank(*refs):
        for ref in refs:
            ref[...] = jnp.zeros(ref.shape, F32)

    for load in loads[:4]:
        load.wait()
    put_one_hot(tab0.at[0], lists_in[0:1, :])
    state = rows8(pos_in[...], vel_in[...], mass_in[...])
    send_a[...] = pick(state, tab0[0])

    pl.semaphore_wait(barrier, awaited)

    def tell(semaphore, peer):
        pl.semaphore_signal(semaphore, inc=1, device_id=(peer,), device_id_type=MESH)

    @pl.when(high)
    def _():
        send(18, 19, 20, 21)
        for k in range(4):
            tell(far_sem.at[k], routes[k][2])
        send(0, 1, 2, 3)
        tell(near_sem, flipped(me, near))

    pl.when(upper)(lambda: tell(seen_sem, beyond))

    send(23)

    @pl.when(hailing)
    def _():
        for k in range(4):
            tell(edge_sem.at[k], flipped(beyond, far | masks[k]))

    @pl.when(served)
    def _():
        for k in range(4):
            tell(hail_sem.at[k], flipped(me - 1, far | masks[k]) + 1)

    send(4, 5)
    pl.when(low)(lambda: send(6))
    ones = jnp.ones((8, half), F32)

    def keep(table):
        return 1.0 - spread(ones, table)[:1]

    kept = state * keep(tab0[0])
    send_k[...] = kept
    send(7, 8)
    pl.when(low)(lambda: send(9))

    @pl.when(high)
    def _():
        pl.semaphore_wait(near_sem, 1)
        send(6, 9)

    pl.when(me < 1)(lambda: blank(recv_r.at[0], recv_c.at[0], recv_f.at[0]))
    pl.when(me > count - 2)(lambda: blank(recv_r.at[1], recv_c.at[1], recv_f.at[1]))
    pl.when(me < 2)(lambda: blank(recv_c.at[2]))
    pl.when(me > count - 3)(lambda: blank(recv_c.at[3]))

    loads[4].wait()
    loads[5].wait()
    rim_row = rim_in[...]
    put_one_hot(tab1.at[0], lists_in[1:2, :])
    put_one_hot(tab2.at[0], lists_in[2:3, :])
    put_one_hot(rim_tab, rim_row)
    first, second = pair_in[0:1, :], pair_in[1:2, :]

    def touch(slot):
        return (jnp.where(slot == first, 1.0, 0.0) - jnp.where(slot == second, 1.0, 0.0)).astype(
            BF16
        )

    def put_ends(i, carry):
        slot = lax.broadcasted_iota(jnp.int32, (32, contacts), 0) + i * 32
        ends[pl.ds(pl.multiple_of(i * 32, 32), 32), :] = touch(slot)
        return carry

    extent = grains + 2 * width
    lax.fori_loop(0, extent // 32, put_ends, 0)
    square = lax.broadcasted_iota(jnp.int32, (width, width), 0) == lax.broadcasted_iota(
        jnp.int32, (width, width), 1
    )
    rim_column = jnp.sum(jnp.where(square, rim_row, 0), axis=1, keepdims=True)
    for i in range(0, width, 32):
        ends[extent + i : extent + i + 32, :] = touch(rim_column[i : i + 32])

    loads[6].wait()
    eye = lax.broadcasted_iota(jnp.int32, (tile, tile), 0) == lax.broadcasted_iota(
        jnp.int32, (tile, tile), 1
    )
    diags = []
    for t in range(tiles):
        block = tiles_in[t]
        head = block.astype(BF16)
        tiles_hi[t * tile : (t + 1) * tile, :] = head
        tiles_lo[t * tile : (t + 1) * tile, :] = (block - head.astype(F32)).astype(BF16)
        diags.append(jnp.sum(jnp.where(eye, block, 0.0), axis=0, keepdims=True))
    diag = jnp.concatenate(diags, axis=1)
    own_tile = lax.broadcasted_iota(jnp.int32, (tiles, contacts), 0) == (
        lax.broadcasted_iota(jnp.int32, (tiles, contacts), 1) // tile
    )

    def coupled(lam):
        table = jnp.concatenate(
            [lam[:, t * tile : (t + 1) * tile] for t in range(tiles)], axis=0
        )
        product = spread(table, tiles_hi[...]) + spread(table, tiles_lo[...])
        return jnp.sum(jnp.where(own_tile, product, 0.0), axis=0, keepdims=True)

    lam = jnp.zeros((1, contacts), F32)
    pull = coupled(lam)

    code_row = lax.broadcasted_iota(jnp.int32, (8, half), 0)
    order = lax.broadcasted_iota(jnp.int32, (8, half), 1).astype(F32) + 1.0

    def coded(k, rows):
        codes = spread(jnp.where(code_row == k, order, 0.0), tab0[k])
        return jnp.concatenate([rows, codes], axis=0)

    def answer():
        for k in range(4):
            pl.semaphore_wait(far_sem.at[k], 1)
            send(k)

    def carry():
        receive(23)
        for k in range(4):

            @pl.when(carried[k])
            def _():
                pl.semaphore_wait(hail_sem.at[k], 1)
                copies[24 + k].start()

    pl.when(both(low, me >= early))(answer)
    pl.when(both(carrier, me >= early))(carry)
    parts = [coded(0, kept)]
    for k in (1, 2, 3):
        receive(3 + k)
        put_one_hot(tab0.at[k], recv_l[k - 1, 0:1, :])
        put_one_hot(tab1.at[k], recv_l[k - 1, 1:2, :])
        if k == 1:
            put_one_hot(tab2.at[1], recv_l[0, 2:3, :])
        receive(6 + k)
        parts.append(coded(k, recv_k[k - 1]))
    pair = [
        parts[k] * keep(tab1[k]) + spread(pick(parts[k + 2], tab1[k + 2]), tab1[k])
        for k in (0, 1)
    ]
    state = pair[0] * keep(tab2[0]) + spread(pick(pair[1], tab2[1]), tab2[0])
    edge = pick(state, rim_tab[...])
    send_e[...] = edge
    pl.when(lower)(lambda: pl.semaphore_wait(seen_sem, 1))
    send(22)
    for k in range(4):
        put_one_hot(
            edge_tab.at[k * half : (k + 1) * half, :], edge[8 + k : 9 + k].astype(jnp.int32), 1
        )
        put_one_hot(
            slot_tab.at[k * half : (k + 1) * half, :], state[8 + k : 9 + k].astype(jnp.int32), 1
        )

    pl.when(me < early)(answer)
    pl.when(both(carrier, me < early))(carry)
    for k in range(4):

        @pl.when(hailed[k])
        def _():
            pl.semaphore_wait(edge_sem.at[k], 1)
            copies[18 + k].start()

    receive(2, 3, 1, 0)
    arrived = split(jnp.concatenate([recv_a[k] for k in range(4)], axis=1))
    edge = edge[:8] + join(jnp.dot(arrived, edge_tab[...], preferred_element_type=F32))
    send_r[...] = edge
    send(10, 11)
    state = state[:8] + join(jnp.dot(arrived, slot_tab[...], preferred_element_type=F32))
    vel, mass = state[3:6], state[6:7]
    gathered = pick(state, ends[:grains, :])

    @pl.when(mine)
    def _():
        receive(22)
        for k in range(4):
            put_one_hot(
                cross_tab.at[k * half : (k + 1) * half, :],
                recv_e[8 + k : 9 + k, :].astype(jnp.int32), 1,
            )
        receive(20, 21, 19, 18, 26, 27, 25, 24)
        seen = split(jnp.concatenate([recv_x[k] for k in range(4)], axis=1))
        recv_r[top.astype(jnp.int32)] = recv_e[:8] + join(
            jnp.dot(seen, cross_tab[...], preferred_element_type=F32)
        )

    receive(10, 11)
    left, right = recv_r[0], recv_r[1]
    gathered += pick(jnp.concatenate([left, right], axis=1), ends[grains:extent, :])
    normal = gathered[0:3]
    speed = jnp.sum(normal * gathered[3:6], axis=0, keepdims=True)
    lam = jnp.maximum(0.0, lam - (pull + speed) / diag)
    force = rows8(normal * lam)
    partial = spread(force, ends[grains:, :])[0:3]
    ghost_left, ghost_right = partial[:, :width], partial[:, width : 2 * width]
    at_rim = partial[:, 2 * width :]
    send_c[0] = rows8(ghost_right, at_rim)
    send_c[1] = rows8(ghost_left, at_rim)
    send(12, 13, 14, 15)
    local = spread(force, ends[:grains, :])[0:3]
    base = pick(rows8(vel + mass * local), ends[:grains, :])[0:3]
    pull = coupled(lam)

    receive(12, 13, 14, 15)
    incoming = edge[6:7] * (recv_c[0, 0:3] + recv_c[1, 0:3])
    fresh_left = left[3:6] + left[6:7] * (recv_c[0, 3:6] + ghost_left + recv_c[2, 0:3])
    fresh_right = right[3:6] + right[6:7] * (recv_c[1, 3:6] + ghost_right + recv_c[3, 0:3])
    relative = base + pick(
        rows8(jnp.concatenate([fresh_left, fresh_right, incoming], axis=1)), ends[grains:, :]
    )[0:3]
    speed = jnp.sum(normal * relative, axis=0, keepdims=True)
    lam = jnp.maximum(0.0, lam - (pull + speed) / diag)
    force = rows8(normal * lam)
    partial = spread(force, ends[grains:extent, :])
    send_f[0] = partial[:, width:]
    send_f[1] = partial[:, :width]
    send(16, 17)
    lam_out[...] = lam
    base = vel + mass * spread(force, ends[:grains, :])[0:3]

    receive(16, 17)
    vel_out[...] = base + mass * spread(recv_f[0] + recv_f[1], rim_tab[...])[0:3]
    for i in range(MESSAGES):
        guarded(copies[i].wait_send, routes[i][3])


def settle(vel_ref, lam_ref, vel_out, lam_out, sem):
    moves = [
        pltpu.make_async_copy(vel_ref, vel_out, sem.at[0]),
        pltpu.make_async_copy(lam_ref, lam_out, sem.at[1]),
    ]
    for move in moves:
        move.start()
    for move in moves:
        move.wait()


def body(count, positions, velocity, inv_mass, swap_lists, rim_list, contact_pair, delassus):
    grains = positions.shape[1]
    half = swap_lists.shape[1]
    width = rim_list.shape[0]
    contacts = contact_pair.shape[1]
    tiles, tile = delassus.shape[:2]
    args = (
        positions, velocity, inv_mass.reshape(1, grains), swap_lists, rim_list.reshape(1, width),
        contact_pair, delassus,
    )
    args = tuple(pltpu.with_memory_space_constraint(arg, pltpu.HBM) for arg in args)

    current, lam = pl.pallas_call(
        lambda *refs: kernel(count, *refs),
        out_shape=(
            jax.ShapeDtypeStruct((3, grains), F32),
            jax.ShapeDtypeStruct((1, contacts), F32),
        ),
        in_specs=[pl.BlockSpec(memory_space=pltpu.HBM)] * len(args),
        out_specs=(
            pl.BlockSpec(memory_space=pltpu.VMEM),
            pl.BlockSpec(memory_space=pltpu.VMEM),
        ),
        scratch_shapes=[pltpu.VMEM(arg.shape, arg.dtype) for arg in args]
        + [
            pltpu.VMEM((grains + 3 * width, contacts), BF16),
            pltpu.VMEM((4, grains, half), BF16),
            pltpu.VMEM((4, grains, half), BF16),
            pltpu.VMEM((2, grains, half), BF16),
            pltpu.VMEM((grains, width), BF16),
            pltpu.VMEM((4 * half, grains), BF16),
            pltpu.VMEM((4 * half, width), BF16),
            pltpu.VMEM((4 * half, width), BF16),
            pltpu.VMEM((contacts, tile), BF16),
            pltpu.VMEM((contacts, tile), BF16),
            pltpu.VMEM((8, half), F32),
            pltpu.VMEM((8, grains), F32),
            pltpu.VMEM((8, width), F32),
            pltpu.VMEM((2, 8, width), F32),
            pltpu.VMEM((2, 8, width), F32),
            pltpu.VMEM((16, width), F32),
            pltpu.VMEM((4, 8, half), F32),
            pltpu.VMEM((3, 3, half), jnp.int32),
            pltpu.VMEM((3, 8, grains), F32),
            pltpu.VMEM((2, 8, width), F32),
            pltpu.VMEM((4, 8, width), F32),
            pltpu.VMEM((2, 8, width), F32),
            pltpu.VMEM((4, 8, half), F32),
            pltpu.VMEM((16, width), F32),
            pltpu.VMEM((8, half), F32),
            pltpu.SemaphoreType.DMA((len(args),)),
            pltpu.SemaphoreType.DMA((MESSAGES,)),
            pltpu.SemaphoreType.DMA((MESSAGES,)),
            pltpu.SemaphoreType.REGULAR((4,)),
            pltpu.SemaphoreType.REGULAR((4,)),
            pltpu.SemaphoreType.REGULAR((4,)),
            pltpu.SemaphoreType.REGULAR,
            pltpu.SemaphoreType.REGULAR,
        ],
        compiler_params=pltpu.CompilerParams(
            collective_id=0, has_side_effects=True, vmem_limit_bytes=32 << 20
        ),
        name="contact_step",
    )(*args)
    current, lam = pl.pallas_call(
        settle,
        out_shape=(
            jax.ShapeDtypeStruct((3, grains), F32),
            jax.ShapeDtypeStruct((1, contacts), F32),
        ),
        in_specs=[pl.BlockSpec(memory_space=pl.ANY)] * 2,
        out_specs=(
            pl.BlockSpec(memory_space=pltpu.HBM), pl.BlockSpec(memory_space=pltpu.HBM)
        ),
        scratch_shapes=[pltpu.SemaphoreType.DMA((2,))],
        name="settle",
    )(
        pltpu.with_memory_space_constraint(current, pltpu.VMEM),
        pltpu.with_memory_space_constraint(lam, pltpu.VMEM),
    )
    return current, lam.reshape(contacts)


def solution(mesh):
    count = mesh.shape["parts"]
    in_specs = (
        P(None, "parts"),
        P(None, "parts"),
        P("parts"),
        P(None, "parts"),
        P("parts"),
        P(None, "parts"),
        P("parts", None, None),
    )
    out_specs = (P(None, "parts"), P("parts"))
    return jax.shard_map(
        lambda *args: body(count, *args),
        mesh=mesh, in_specs=in_specs, out_specs=out_specs, check_vma=False,
    )
```

```python
import functools

import jax
import jax.numpy as jnp
from jax import lax
from jax.experimental import pallas as pl
from jax.experimental.pallas import tpu as pltpu
from jax.sharding import PartitionSpec as P

MESH = pl.DeviceIdType.MESH
F32 = jnp.float32
BF16 = jnp.bfloat16
MESSAGES = 28


def split(x):
    head = x.astype(BF16).astype(F32)
    return jnp.concatenate([head, x - head], axis=0).astype(BF16)


def join(y):
    half = y.shape[0] // 2
    return y[:half] + y[half:]


def pick(x, table):
    return join(jnp.dot(split(x), table, preferred_element_type=F32))


def spread(x, table):
    return join(
        lax.dot_general(split(x), table, (((1,), (1,)), ((), ())), preferred_element_type=F32)
    )


def rows8(*pieces):
    have = sum(piece.shape[0] for piece in pieces)
    if have < 8:
        pieces += (jnp.zeros((8 - have, pieces[0].shape[1]), F32),)
    return jnp.concatenate(pieces, axis=0)


def put_one_hot(table, row, base=0):
    extent, width = table.shape
    block = 64

    def step(i, carry):
        slot = lax.broadcasted_iota(jnp.int32, (block, width), 0) + (i * block + base)
        table[pl.ds(pl.multiple_of(i * block, block), block), :] = jnp.where(
            slot == row, 1.0, 0.0
        ).astype(BF16)
        return carry

    lax.fori_loop(0, extent // block, step, 0)


def kernel(
    count,
    pos_hbm, vel_hbm, mass_hbm, lists_hbm, rim_hbm, pair_hbm, tiles_hbm,
    vel_out, lam_out,
    pos_in, vel_in, mass_in, lists_in, rim_in, pair_in, tiles_in,
    ends, tab0, tab1, tab2, rim_tab, slot_tab, edge_tab, cross_tab, tiles_hi, tiles_lo,
    send_a, send_k, send_r, send_c, send_f, send_e,
    recv_a, recv_l, recv_k, recv_r, recv_c, recv_f, recv_x, recv_e, recv_p,
    in_sem, send_sem, recv_sem, far_sem, edge_sem, hail_sem, near_sem, seen_sem,
):
    grains = pos_in.shape[1]
    half = lists_in.shape[1]
    width = rim_in.shape[1]
    contacts = pair_in.shape[1]
    tiles, tile = tiles_in.shape[:2]
    bits = count.bit_length() - 1
    far, mid, near = (1 << (bits - 1 - level) for level in range(3))
    masks = (0, near, mid, mid | near)
    plane = count // 16
    me = lax.axis_index("parts")
    high = me >= far
    low = me < far

    def shifted(base, by):
        return lax.rem(base + (by + count), count)

    def flipped(base, mask):
        return lax.bitwise_xor(base, jnp.int32(mask))

    def both(*conditions):
        return functools.reduce(jnp.logical_and, conditions)

    def inside(by):
        return me >= -by if by < 0 else me < count - by

    spot = lax.rem(me, plane)
    top, bottom = spot == plane - 1, spot == 0
    edge_side = jnp.where(top, 1, -1)
    beyond = me + edge_side
    across = jnp.logical_and(
        jnp.logical_or(top, bottom), jnp.logical_and(beyond >= 0, beyond < count)
    )
    relays = [flipped(me, far | mask) + edge_side for mask in masks]
    early = far // 2

    def quick(part):
        return functools.reduce(
            jnp.logical_or, [part <= early, part == far - 1, part > far, part == early + plane]
        )

    mine, theirs = both(across, quick(me)), both(across, quick(beyond))
    relayed = [
        both(
            to >= 0,
            jnp.logical_or(
                both(high, jnp.logical_or(top, bottom), to < far - 1, quick(to)),
                both(low, bottom),
            ),
        )
        for to in relays
    ]
    carrier = both(bottom, me > 0, me <= far)
    carries = [flipped(me - carrier.astype(jnp.int32), far | mask) + 1 for mask in masks]
    carried = [both(carrier, to < count) for to in carries]
    served = both(bottom, me > far)

    loads = [
        pltpu.make_async_copy(src, dst, in_sem.at[i])
        for i, (src, dst) in enumerate(
            [
                (lists_hbm, lists_in), (pos_hbm, pos_in), (vel_hbm, vel_in), (mass_hbm, mass_in),
                (rim_hbm, rim_in), (pair_hbm, pair_in), (tiles_hbm, tiles_in),
            ]
        )
    ]
    for load in loads[:4]:
        load.start()

    barrier = pltpu.get_barrier_semaphore()

    def greet(peer):
        pl.semaphore_signal(barrier, inc=1, device_id=(peer,), device_id_type=MESH)

    @pl.when(low)
    def _():
        for mask in masks:
            greet(flipped(me, far | mask))

    for mask in (near, mid):
        greet(flipped(me, mask))
    pl.when(low)(lambda: greet(flipped(me, masks[3])))
    awaited = 3 + 3 * high.astype(jnp.int32)
    lower, upper = both(bottom, across), both(top, across)
    for by, skipped, excused in ((1, upper, False), (-1, False, lower)):
        pl.when(both(inside(by), jnp.logical_not(skipped)))(
            functools.partial(greet, shifted(me, by))
        )
        awaited += both(inside(by), jnp.logical_not(excused)).astype(jnp.int32)
    hailing = both(upper, beyond >= far)
    awaited += 4 * hailing.astype(jnp.int32)
    hailed = [jnp.logical_and(jnp.logical_and(low, bottom), condition) for condition in relayed]
    for to, condition in zip(relays + carries, hailed + carried):
        pl.when(condition)(functools.partial(greet, to))
    awaited += 4 * served.astype(jnp.int32)

    @pl.when(both(mine, me < far - 1))
    def _():
        for mask in masks:
            greet(flipped(beyond, far | mask))

    for condition in relayed:
        awaited += jnp.logical_and(high, condition).astype(jnp.int32)

    routes = [(send_a, recv_a.at[k], flipped(me, far | masks[k]), None, None) for k in range(4)]
    routes += [
        (src, dst.at[k - 1], flipped(me, masks[k]), None, None)
        for src, dst in ((lists_in, recv_l), (send_k, recv_k))
        for k in (1, 2, 3)
    ]
    routes += [
        (src, dst, shifted(me, by), inside(by), inside(-by))
        for src, dst, by in (
            (send_r, recv_r.at[0], 1),
            (send_r, recv_r.at[1], -1),
            (send_c.at[0], recv_c.at[0], 1),
            (send_c.at[1], recv_c.at[1], -1),
            (send_c.at[0], recv_c.at[2], 2),
            (send_c.at[1], recv_c.at[3], -2),
            (send_f.at[0], recv_f.at[0], 1),
            (send_f.at[1], recv_f.at[1], -1),
        )
    ]
    for i, out_gate, in_gate in ((10, top, bottom), (11, bottom, top)):
        routes[i] = routes[i][:3] + tuple(
            both(condition, jnp.logical_not(both(gate, hurried)))
            for condition, gate, hurried in zip(
                routes[i][3:], (out_gate, in_gate), (theirs, mine)
            )
        )
    direct = both(mine, jnp.logical_not(served))
    routes += [(send_a, recv_x.at[k], relays[k], relayed[k], direct) for k in range(4)]
    routes += [(send_e, recv_e, beyond, theirs, mine)]
    routes += [(send_a, recv_p, beyond, both(top, low), carrier)]
    routes += [(recv_p, recv_x.at[k], carries[k], carried[k], served) for k in range(4)]
    copies = [
        pltpu.make_async_remote_copy(
            src_ref=src, dst_ref=dst, send_sem=send_sem.at[i], recv_sem=recv_sem.at[i],
            device_id=(target,), device_id_type=MESH,
        )
        for i, (src, dst, target, _, _) in enumerate(routes)
    ]

    def guarded(action, condition):
        if condition is None:
            action()
        else:
            pl.when(condition)(action)

    def send(*which):
        for i in which:
            guarded(copies[i].start, routes[i][3])

    def receive(*which):
        for i in which:
            guarded(copies[i].wait_recv, routes[i][4])

    def settled(*which):
        for i in which:
            guarded(copies[i].wait_send, routes[i][3])

    def blank(*refs):
        for ref in refs:
            ref[...] = jnp.zeros(ref.shape, F32)

    for load in loads[:4]:
        load.wait()
    put_one_hot(tab0.at[0], lists_in[0:1, :])
    state = rows8(pos_in[...], vel_in[...], mass_in[...])
    send_a[...] = pick(state, tab0[0])

    pl.semaphore_wait(barrier, awaited)

    def tell(semaphore, peer):
        pl.semaphore_signal(semaphore, inc=1, device_id=(peer,), device_id_type=MESH)

    @pl.when(high)
    def _():
        send(18, 19, 20, 21)
        for k in range(4):
            tell(far_sem.at[k], routes[k][2])
        send(0, 1, 2, 3)
        tell(near_sem, flipped(me, near))

    pl.when(upper)(lambda: tell(seen_sem, beyond))

    send(23)

    @pl.when(hailing)
    def _():
        for k in range(4):
            tell(edge_sem.at[k], flipped(beyond, far | masks[k]))

    @pl.when(served)
    def _():
        for k in range(4):
            tell(hail_sem.at[k], flipped(me - 1, far | masks[k]) + 1)

    for load in loads[4:]:
        load.start()
    send(4, 5)
    pl.when(low)(lambda: send(6))
    ones = jnp.ones((8, half), F32)

    def keep(table):
        return 1.0 - spread(ones, table)[:1]

    kept = state * keep(tab0[0])
    send_k[...] = kept
    send(7, 8)
    pl.when(low)(lambda: send(9))

    @pl.when(high)
    def _():
        pl.semaphore_wait(near_sem, 1)
        send(6, 9)

    pl.when(me < 1)(lambda: blank(recv_r.at[0], recv_c.at[0], recv_f.at[0]))
    pl.when(me > count - 2)(lambda: blank(recv_r.at[1], recv_c.at[1], recv_f.at[1]))
    pl.when(me < 2)(lambda: blank(recv_c.at[2]))
    pl.when(me > count - 3)(lambda: blank(recv_c.at[3]))

    loads[4].wait()
    loads[5].wait()
    rim_row = rim_in[...]
    put_one_hot(tab1.at[0], lists_in[1:2, :])
    put_one_hot(tab2.at[0], lists_in[2:3, :])
    put_one_hot(rim_tab, rim_row)
    first, second = pair_in[0:1, :], pair_in[1:2, :]

    def touch(slot):
        return (jnp.where(slot == first, 1.0, 0.0) - jnp.where(slot == second, 1.0, 0.0)).astype(
            BF16
        )

    def put_ends(i, carry):
        slot = lax.broadcasted_iota(jnp.int32, (32, contacts), 0) + i * 32
        ends[pl.ds(pl.multiple_of(i * 32, 32), 32), :] = touch(slot)
        return carry

    extent = grains + 2 * width
    lax.fori_loop(0, extent // 32, put_ends, 0)
    square = lax.broadcasted_iota(jnp.int32, (width, width), 0) == lax.broadcasted_iota(
        jnp.int32, (width, width), 1
    )
    rim_column = jnp.sum(jnp.where(square, rim_row, 0), axis=1, keepdims=True)
    for i in range(0, width, 32):
        ends[extent + i : extent + i + 32, :] = touch(rim_column[i : i + 32])

    loads[6].wait()
    eye = lax.broadcasted_iota(jnp.int32, (tile, tile), 0) == lax.broadcasted_iota(
        jnp.int32, (tile, tile), 1
    )
    diags = []
    for t in range(tiles):
        block = tiles_in[t]
        head = block.astype(BF16)
        tiles_hi[t * tile : (t + 1) * tile, :] = head
        tiles_lo[t * tile : (t + 1) * tile, :] = (block - head.astype(F32)).astype(BF16)
        diags.append(jnp.sum(jnp.where(eye, block, 0.0), axis=0, keepdims=True))
    diag = jnp.concatenate(diags, axis=1)
    own_tile = lax.broadcasted_iota(jnp.int32, (tiles, contacts), 0) == (
        lax.broadcasted_iota(jnp.int32, (tiles, contacts), 1) // tile
    )

    def coupled(lam):
        table = jnp.concatenate(
            [lam[:, t * tile : (t + 1) * tile] for t in range(tiles)], axis=0
        )
        product = spread(table, tiles_hi[...]) + spread(table, tiles_lo[...])
        return jnp.sum(jnp.where(own_tile, product, 0.0), axis=0, keepdims=True)

    lam = jnp.zeros((1, contacts), F32)
    pull = coupled(lam)

    code_row = lax.broadcasted_iota(jnp.int32, (8, half), 0)
    order = lax.broadcasted_iota(jnp.int32, (8, half), 1).astype(F32) + 1.0

    def coded(k, rows):
        codes = spread(jnp.where(code_row == k, order, 0.0), tab0[k])
        return jnp.concatenate([rows, codes], axis=0)

    def answer():
        for k in range(4):
            pl.semaphore_wait(far_sem.at[k], 1)
            send(k)

    def carry():
        receive(23)
        for k in range(4):

            @pl.when(carried[k])
            def _():
                pl.semaphore_wait(hail_sem.at[k], 1)
                copies[24 + k].start()

    pl.when(both(low, me >= early))(answer)
    pl.when(both(carrier, me >= early))(carry)
    parts = [coded(0, kept)]
    for k in (1, 2, 3):
        receive(3 + k)
        put_one_hot(tab0.at[k], recv_l[k - 1, 0:1, :])
        put_one_hot(tab1.at[k], recv_l[k - 1, 1:2, :])
        if k == 1:
            put_one_hot(tab2.at[1], recv_l[0, 2:3, :])
        receive(6 + k)
        parts.append(coded(k, recv_k[k - 1]))
    pair = [
        parts[k] * keep(tab1[k]) + spread(pick(parts[k + 2], tab1[k + 2]), tab1[k])
        for k in (0, 1)
    ]
    state = pair[0] * keep(tab2[0]) + spread(pick(pair[1], tab2[1]), tab2[0])
    edge = pick(state, rim_tab[...])
    send_e[...] = edge
    pl.when(lower)(lambda: pl.semaphore_wait(seen_sem, 1))
    send(22)
    for k in range(4):
        put_one_hot(
            edge_tab.at[k * half : (k + 1) * half, :], edge[8 + k : 9 + k].astype(jnp.int32), 1
        )
        put_one_hot(
            slot_tab.at[k * half : (k + 1) * half, :], state[8 + k : 9 + k].astype(jnp.int32), 1
        )

    pl.when(me < early)(answer)
    pl.when(both(carrier, me < early))(carry)
    for k in range(4):

        @pl.when(hailed[k])
        def _():
            pl.semaphore_wait(edge_sem.at[k], 1)
            copies[18 + k].start()

    receive(2, 3, 1, 0)
    arrived = split(jnp.concatenate([recv_a[k] for k in range(4)], axis=1))
    edge = edge[:8] + join(jnp.dot(arrived, edge_tab[...], preferred_element_type=F32))
    send_r[...] = edge
    send(10, 11)
    state = state[:8] + join(jnp.dot(arrived, slot_tab[...], preferred_element_type=F32))
    vel, mass = state[3:6], state[6:7]
    gathered = pick(state, ends[:grains, :])

    @pl.when(mine)
    def _():
        receive(22)
        for k in range(4):
            put_one_hot(
                cross_tab.at[k * half : (k + 1) * half, :],
                recv_e[8 + k : 9 + k, :].astype(jnp.int32), 1,
            )
        receive(20, 21, 19, 18, 26, 27, 25, 24)
        seen = split(jnp.concatenate([recv_x[k] for k in range(4)], axis=1))
        recv_r[top.astype(jnp.int32)] = recv_e[:8] + join(
            jnp.dot(seen, cross_tab[...], preferred_element_type=F32)
        )

    receive(10, 11)
    left, right = recv_r[0], recv_r[1]
    gathered += pick(jnp.concatenate([left, right], axis=1), ends[grains:extent, :])
    normal = gathered[0:3]
    speed = jnp.sum(normal * gathered[3:6], axis=0, keepdims=True)
    lam = jnp.maximum(0.0, lam - (pull + speed) / diag)
    force = rows8(normal * lam)
    partial = spread(force, ends[grains:, :])[0:3]
    ghost_left, ghost_right = partial[:, :width], partial[:, width : 2 * width]
    at_rim = partial[:, 2 * width :]
    send_c[0] = rows8(ghost_right, at_rim)
    send_c[1] = rows8(ghost_left, at_rim)
    send(12, 13, 14, 15)
    local = spread(force, ends[:grains, :])[0:3]
    base = pick(rows8(vel + mass * local), ends[:grains, :])[0:3]
    pull = coupled(lam)

    receive(12, 13, 14, 15)
    incoming = edge[6:7] * (recv_c[0, 0:3] + recv_c[1, 0:3])
    fresh_left = left[3:6] + left[6:7] * (recv_c[0, 3:6] + ghost_left + recv_c[2, 0:3])
    fresh_right = right[3:6] + right[6:7] * (recv_c[1, 3:6] + ghost_right + recv_c[3, 0:3])
    relative = base + pick(
        rows8(jnp.concatenate([fresh_left, fresh_right, incoming], axis=1)), ends[grains:, :]
    )[0:3]
    speed = jnp.sum(normal * relative, axis=0, keepdims=True)
    lam = jnp.maximum(0.0, lam - (pull + speed) / diag)
    force = rows8(normal * lam)
    partial = spread(force, ends[grains:extent, :])
    send_f[0] = partial[:, width:]
    send_f[1] = partial[:, :width]
    send(16, 17)
    lam_out[...] = lam
    base = vel + mass * spread(force, ends[:grains, :])[0:3]
    settled(*range(16), *range(18, MESSAGES))

    receive(16, 17)
    vel_out[...] = base + mass * spread(recv_f[0] + recv_f[1], rim_tab[...])[0:3]
    settled(16, 17)


def settle(vel_ref, lam_ref, vel_out, lam_out, sem):
    moves = [
        pltpu.make_async_copy(vel_ref, vel_out, sem.at[0]),
        pltpu.make_async_copy(lam_ref, lam_out, sem.at[1]),
    ]
    for move in moves:
        move.start()
    for move in moves:
        move.wait()


def body(count, positions, velocity, inv_mass, swap_lists, rim_list, contact_pair, delassus):
    grains = positions.shape[1]
    half = swap_lists.shape[1]
    width = rim_list.shape[0]
    contacts = contact_pair.shape[1]
    tiles, tile = delassus.shape[:2]
    args = (
        positions, velocity, inv_mass.reshape(1, grains), swap_lists, rim_list.reshape(1, width),
        contact_pair, delassus,
    )
    args = tuple(pltpu.with_memory_space_constraint(arg, pltpu.HBM) for arg in args)

    current, lam = pl.pallas_call(
        lambda *refs: kernel(count, *refs),
        out_shape=(
            jax.ShapeDtypeStruct((3, grains), F32),
            jax.ShapeDtypeStruct((1, contacts), F32),
        ),
        in_specs=[pl.BlockSpec(memory_space=pltpu.HBM)] * len(args),
        out_specs=(
            pl.BlockSpec(memory_space=pltpu.VMEM),
            pl.BlockSpec(memory_space=pltpu.VMEM),
        ),
        scratch_shapes=[pltpu.VMEM(arg.shape, arg.dtype) for arg in args]
        + [
            pltpu.VMEM((grains + 3 * width, contacts), BF16),
            pltpu.VMEM((4, grains, half), BF16),
            pltpu.VMEM((4, grains, half), BF16),
            pltpu.VMEM((2, grains, half), BF16),
            pltpu.VMEM((grains, width), BF16),
            pltpu.VMEM((4 * half, grains), BF16),
            pltpu.VMEM((4 * half, width), BF16),
            pltpu.VMEM((4 * half, width), BF16),
            pltpu.VMEM((contacts, tile), BF16),
            pltpu.VMEM((contacts, tile), BF16),
            pltpu.VMEM((8, half), F32),
            pltpu.VMEM((8, grains), F32),
            pltpu.VMEM((8, width), F32),
            pltpu.VMEM((2, 8, width), F32),
            pltpu.VMEM((2, 8, width), F32),
            pltpu.VMEM((16, width), F32),
            pltpu.VMEM((4, 8, half), F32),
            pltpu.VMEM((3, 3, half), jnp.int32),
            pltpu.VMEM((3, 8, grains), F32),
            pltpu.VMEM((2, 8, width), F32),
            pltpu.VMEM((4, 8, width), F32),
            pltpu.VMEM((2, 8, width), F32),
            pltpu.VMEM((4, 8, half), F32),
            pltpu.VMEM((16, width), F32),
            pltpu.VMEM((8, half), F32),
            pltpu.SemaphoreType.DMA((len(args),)),
            pltpu.SemaphoreType.DMA((MESSAGES,)),
            pltpu.SemaphoreType.DMA((MESSAGES,)),
            pltpu.SemaphoreType.REGULAR((4,)),
            pltpu.SemaphoreType.REGULAR((4,)),
            pltpu.SemaphoreType.REGULAR((4,)),
            pltpu.SemaphoreType.REGULAR,
            pltpu.SemaphoreType.REGULAR,
        ],
        compiler_params=pltpu.CompilerParams(
            collective_id=0, has_side_effects=True, vmem_limit_bytes=32 << 20
        ),
        name="contact_step",
    )(*args)
    current, lam = pl.pallas_call(
        settle,
        out_shape=(
            jax.ShapeDtypeStruct((3, grains), F32),
            jax.ShapeDtypeStruct((1, contacts), F32),
        ),
        in_specs=[pl.BlockSpec(memory_space=pl.ANY)] * 2,
        out_specs=(
            pl.BlockSpec(memory_space=pltpu.HBM), pl.BlockSpec(memory_space=pltpu.HBM)
        ),
        scratch_shapes=[pltpu.SemaphoreType.DMA((2,))],
        name="settle",
    )(
        pltpu.with_memory_space_constraint(current, pltpu.VMEM),
        pltpu.with_memory_space_constraint(lam, pltpu.VMEM),
    )
    return current, lam.reshape(contacts)


def solution(mesh):
    count = mesh.shape["parts"]
    in_specs = (
        P(None, "parts"),
        P(None, "parts"),
        P("parts"),
        P(None, "parts"),
        P("parts"),
        P(None, "parts"),
        P("parts", None, None),
    )
    out_specs = (P(None, "parts"), P("parts"))
    return jax.shard_map(
        lambda *args: body(count, *args),
        mesh=mesh, in_specs=in_specs, out_specs=out_specs, check_vma=False,
    )
```

```python
import functools

import jax
import jax.numpy as jnp
from jax import lax
from jax.experimental import pallas as pl
from jax.experimental.pallas import tpu as pltpu
from jax.sharding import PartitionSpec as P

MESH = pl.DeviceIdType.MESH
F32 = jnp.float32
BF16 = jnp.bfloat16
MESSAGES = 28


def split(x):
    head = x.astype(BF16).astype(F32)
    return jnp.concatenate([head, x - head], axis=0).astype(BF16)


def join(y):
    half = y.shape[0] // 2
    return y[:half] + y[half:]


def pick(x, table):
    return join(jnp.dot(split(x), table, preferred_element_type=F32))


def spread(x, table):
    return join(
        lax.dot_general(split(x), table, (((1,), (1,)), ((), ())), preferred_element_type=F32)
    )


def rows8(*pieces):
    have = sum(piece.shape[0] for piece in pieces)
    if have < 8:
        pieces += (jnp.zeros((8 - have, pieces[0].shape[1]), F32),)
    return jnp.concatenate(pieces, axis=0)


def put_one_hot(table, row, base=0):
    extent, width = table.shape
    block = 64

    def step(i, carry):
        slot = lax.broadcasted_iota(jnp.int32, (block, width), 0) + (i * block + base)
        table[pl.ds(pl.multiple_of(i * block, block), block), :] = jnp.where(
            slot == row, 1.0, 0.0
        ).astype(BF16)
        return carry

    lax.fori_loop(0, extent // block, step, 0)


def kernel(
    count,
    pos_hbm, vel_hbm, mass_hbm, lists_hbm, rim_hbm, pair_hbm, tiles_hbm,
    vel_out, lam_out,
    pos_in, vel_in, mass_in, lists_in, rim_in, pair_in, tiles_in,
    ends, tab0, tab1, tab2, rim_tab, slot_tab, edge_tab, cross_tab, tiles_hi, tiles_lo,
    send_a, send_k, send_r, send_c, send_f, send_e,
    recv_a, recv_l, recv_k, recv_r, recv_c, recv_f, recv_x, recv_e, recv_p,
    in_sem, send_sem, recv_sem, far_sem, edge_sem, hail_sem, near_sem, seen_sem,
):
    grains = pos_in.shape[1]
    half = lists_in.shape[1]
    width = rim_in.shape[1]
    contacts = pair_in.shape[1]
    tiles, tile = tiles_in.shape[:2]
    bits = count.bit_length() - 1
    far, mid, near = (1 << (bits - 1 - level) for level in range(3))
    masks = (0, near, mid, mid | near)
    plane = count // 16
    me = lax.axis_index("parts")
    high = me >= far
    low = me < far

    def shifted(base, by):
        return lax.rem(base + (by + count), count)

    def flipped(base, mask):
        return lax.bitwise_xor(base, jnp.int32(mask))

    def both(*conditions):
        return functools.reduce(jnp.logical_and, conditions)

    def inside(by):
        return me >= -by if by < 0 else me < count - by

    spot = lax.rem(me, plane)
    top, bottom = spot == plane - 1, spot == 0
    edge_side = jnp.where(top, 1, -1)
    beyond = me + edge_side
    across = jnp.logical_and(
        jnp.logical_or(top, bottom), jnp.logical_and(beyond >= 0, beyond < count)
    )
    relays = [flipped(me, far | mask) + edge_side for mask in masks]
    early = far // 2

    def quick(part):
        return functools.reduce(
            jnp.logical_or, [part <= early, part == far - 1, part > far, part == early + plane]
        )

    mine, theirs = both(across, quick(me)), both(across, quick(beyond))
    relayed = [
        both(
            to >= 0,
            jnp.logical_or(
                both(high, jnp.logical_or(top, bottom), to < far - 1, quick(to)),
                both(low, bottom),
            ),
        )
        for to in relays
    ]
    carrier = both(bottom, me > 0, me <= far)
    carries = [flipped(me - carrier.astype(jnp.int32), far | mask) + 1 for mask in masks]
    carried = [both(carrier, to < count) for to in carries]
    served = both(bottom, me > far)

    loads = [
        pltpu.make_async_copy(src, dst, in_sem.at[i])
        for i, (src, dst) in enumerate(
            [
                (lists_hbm, lists_in), (pos_hbm, pos_in), (vel_hbm, vel_in), (mass_hbm, mass_in),
                (rim_hbm, rim_in), (pair_hbm, pair_in), (tiles_hbm, tiles_in),
            ]
        )
    ]
    for load in loads:
        load.start()

    barrier = pltpu.get_barrier_semaphore()

    def greet(peer):
        pl.semaphore_signal(barrier, inc=1, device_id=(peer,), device_id_type=MESH)

    @pl.when(low)
    def _():
        for mask in masks:
            greet(flipped(me, far | mask))

    for mask in (near, mid):
        greet(flipped(me, mask))
    pl.when(low)(lambda: greet(flipped(me, masks[3])))
    awaited = 3 + 3 * high.astype(jnp.int32)
    lower, upper = both(bottom, across), both(top, across)
    for by, skipped, excused in ((1, upper, False), (-1, False, lower)):
        pl.when(both(inside(by), jnp.logical_not(skipped)))(
            functools.partial(greet, shifted(me, by))
        )
        awaited += both(inside(by), jnp.logical_not(excused)).astype(jnp.int32)
    hailing = both(upper, beyond >= far)
    awaited += 4 * hailing.astype(jnp.int32)
    hailed = [jnp.logical_and(jnp.logical_and(low, bottom), condition) for condition in relayed]
    for to, condition in zip(relays + carries, hailed + carried):
        pl.when(condition)(functools.partial(greet, to))
    awaited += 4 * served.astype(jnp.int32)

    @pl.when(both(mine, me < far - 1))
    def _():
        for mask in masks:
            greet(flipped(beyond, far | mask))

    for condition in relayed:
        awaited += jnp.logical_and(high, condition).astype(jnp.int32)

    routes = [(send_a, recv_a.at[k], flipped(me, far | masks[k]), None, None) for k in range(4)]
    routes += [
        (src, dst.at[k - 1], flipped(me, masks[k]), None, None)
        for src, dst in ((lists_in, recv_l), (send_k, recv_k))
        for k in (1, 2, 3)
    ]
    routes += [
        (src, dst, shifted(me, by), inside(by), inside(-by))
        for src, dst, by in (
            (send_r, recv_r.at[0], 1),
            (send_r, recv_r.at[1], -1),
            (send_c.at[0], recv_c.at[0], 1),
            (send_c.at[1], recv_c.at[1], -1),
            (send_c.at[0], recv_c.at[2], 2),
            (send_c.at[1], recv_c.at[3], -2),
            (send_f.at[0], recv_f.at[0], 1),
            (send_f.at[1], recv_f.at[1], -1),
        )
    ]
    for i, out_gate, in_gate in ((10, top, bottom), (11, bottom, top)):
        routes[i] = routes[i][:3] + tuple(
            both(condition, jnp.logical_not(both(gate, hurried)))
            for condition, gate, hurried in zip(
                routes[i][3:], (out_gate, in_gate), (theirs, mine)
            )
        )
    direct = both(mine, jnp.logical_not(served))
    routes += [(send_a, recv_x.at[k], relays[k], relayed[k], direct) for k in range(4)]
    routes += [(send_e, recv_e, beyond, theirs, mine)]
    routes += [(send_a, recv_p, beyond, both(top, low), carrier)]
    routes += [(recv_p, recv_x.at[k], carries[k], carried[k], served) for k in range(4)]
    copies = [
        pltpu.make_async_remote_copy(
            src_ref=src, dst_ref=dst, send_sem=send_sem.at[i], recv_sem=recv_sem.at[i],
            device_id=(target,), device_id_type=MESH,
        )
        for i, (src, dst, target, _, _) in enumerate(routes)
    ]

    def guarded(action, condition):
        if condition is None:
            action()
        else:
            pl.when(condition)(action)

    def send(*which):
        for i in which:
            guarded(copies[i].start, routes[i][3])

    def receive(*which):
        for i in which:
            guarded(copies[i].wait_recv, routes[i][4])

    def settled(*which):
        for i in which:
            guarded(copies[i].wait_send, routes[i][3])

    def blank(*refs):
        for ref in refs:
            ref[...] = jnp.zeros(ref.shape, F32)

    for load in loads[:4]:
        load.wait()
    put_one_hot(tab0.at[0], lists_in[0:1, :])
    state = rows8(pos_in[...], vel_in[...], mass_in[...])
    send_a[...] = pick(state, tab0[0])

    pl.semaphore_wait(barrier, awaited)

    def tell(semaphore, peer):
        pl.semaphore_signal(semaphore, inc=1, device_id=(peer,), device_id_type=MESH)

    @pl.when(high)
    def _():
        send(18, 19, 20, 21)
        for k in range(4):
            tell(far_sem.at[k], routes[k][2])
        send(0, 1, 2, 3)
        tell(near_sem, flipped(me, near))

    pl.when(upper)(lambda: tell(seen_sem, beyond))

    send(23)

    @pl.when(hailing)
    def _():
        for k in range(4):
            tell(edge_sem.at[k], flipped(beyond, far | masks[k]))

    @pl.when(served)
    def _():
        for k in range(4):
            tell(hail_sem.at[k], flipped(me - 1, far | masks[k]) + 1)

    send(4, 5)
    pl.when(low)(lambda: send(6))
    ones = jnp.ones((8, half), F32)

    def keep(table):
        return 1.0 - spread(ones, table)[:1]

    kept = state * keep(tab0[0])
    send_k[...] = kept
    send(7, 8)
    pl.when(low)(lambda: send(9))

    @pl.when(high)
    def _():
        pl.semaphore_wait(near_sem, 1)
        send(6, 9)

    pl.when(me < 1)(lambda: blank(recv_r.at[0], recv_c.at[0], recv_f.at[0]))
    pl.when(me > count - 2)(lambda: blank(recv_r.at[1], recv_c.at[1], recv_f.at[1]))
    pl.when(me < 2)(lambda: blank(recv_c.at[2]))
    pl.when(me > count - 3)(lambda: blank(recv_c.at[3]))

    loads[4].wait()
    loads[5].wait()
    rim_row = rim_in[...]
    put_one_hot(tab1.at[0], lists_in[1:2, :])
    put_one_hot(tab2.at[0], lists_in[2:3, :])
    put_one_hot(rim_tab, rim_row)
    first, second = pair_in[0:1, :], pair_in[1:2, :]

    def touch(slot):
        return (jnp.where(slot == first, 1.0, 0.0) - jnp.where(slot == second, 1.0, 0.0)).astype(
            BF16
        )

    def put_ends(i, carry):
        slot = lax.broadcasted_iota(jnp.int32, (32, contacts), 0) + i * 32
        ends[pl.ds(pl.multiple_of(i * 32, 32), 32), :] = touch(slot)
        return carry

    extent = grains + 2 * width
    lax.fori_loop(0, extent // 32, put_ends, 0)
    square = lax.broadcasted_iota(jnp.int32, (width, width), 0) == lax.broadcasted_iota(
        jnp.int32, (width, width), 1
    )
    rim_column = jnp.sum(jnp.where(square, rim_row, 0), axis=1, keepdims=True)
    for i in range(0, width, 32):
        ends[extent + i : extent + i + 32, :] = touch(rim_column[i : i + 32])

    loads[6].wait()
    eye = lax.broadcasted_iota(jnp.int32, (tile, tile), 0) == lax.broadcasted_iota(
        jnp.int32, (tile, tile), 1
    )
    diags = []
    for t in range(tiles):
        block = tiles_in[t]
        head = block.astype(BF16)
        tiles_hi[t * tile : (t + 1) * tile, :] = head
        tiles_lo[t * tile : (t + 1) * tile, :] = (block - head.astype(F32)).astype(BF16)
        diags.append(jnp.sum(jnp.where(eye, block, 0.0), axis=0, keepdims=True))
    diag = jnp.concatenate(diags, axis=1)
    own_tile = lax.broadcasted_iota(jnp.int32, (tiles, contacts), 0) == (
        lax.broadcasted_iota(jnp.int32, (tiles, contacts), 1) // tile
    )

    def coupled(lam):
        table = jnp.concatenate(
            [lam[:, t * tile : (t + 1) * tile] for t in range(tiles)], axis=0
        )
        product = spread(table, tiles_hi[...]) + spread(table, tiles_lo[...])
        return jnp.sum(jnp.where(own_tile, product, 0.0), axis=0, keepdims=True)

    lam = jnp.zeros((1, contacts), F32)
    pull = coupled(lam)

    code_row = lax.broadcasted_iota(jnp.int32, (8, half), 0)
    order = lax.broadcasted_iota(jnp.int32, (8, half), 1).astype(F32) + 1.0

    def coded(k, rows):
        codes = spread(jnp.where(code_row == k, order, 0.0), tab0[k])
        return jnp.concatenate([rows, codes], axis=0)

    def answer():
        for k in range(4):
            pl.semaphore_wait(far_sem.at[k], 1)
            send(k)

    def carry():
        receive(23)
        for k in range(4):

            @pl.when(carried[k])
            def _():
                pl.semaphore_wait(hail_sem.at[k], 1)
                copies[24 + k].start()

    pl.when(both(low, me >= early))(answer)
    pl.when(both(carrier, me >= early))(carry)
    parts = [coded(0, kept)]
    for k in (1, 2, 3):
        receive(3 + k)
        put_one_hot(tab0.at[k], recv_l[k - 1, 0:1, :])
        put_one_hot(tab1.at[k], recv_l[k - 1, 1:2, :])
        if k == 1:
            put_one_hot(tab2.at[1], recv_l[0, 2:3, :])
        receive(6 + k)
        parts.append(coded(k, recv_k[k - 1]))
    pair = [
        parts[k] * keep(tab1[k]) + spread(pick(parts[k + 2], tab1[k + 2]), tab1[k])
        for k in (0, 1)
    ]
    state = pair[0] * keep(tab2[0]) + spread(pick(pair[1], tab2[1]), tab2[0])
    edge = pick(state, rim_tab[...])
    send_e[...] = edge
    pl.when(lower)(lambda: pl.semaphore_wait(seen_sem, 1))
    send(22)
    for k in range(4):
        put_one_hot(
            edge_tab.at[k * half : (k + 1) * half, :], edge[8 + k : 9 + k].astype(jnp.int32), 1
        )
        put_one_hot(
            slot_tab.at[k * half : (k + 1) * half, :], state[8 + k : 9 + k].astype(jnp.int32), 1
        )

    pl.when(me < early)(answer)
    pl.when(both(carrier, me < early))(carry)
    for k in range(4):

        @pl.when(hailed[k])
        def _():
            pl.semaphore_wait(edge_sem.at[k], 1)
            copies[18 + k].start()

    receive(2, 3, 1, 0)
    arrived = split(jnp.concatenate([recv_a[k] for k in range(4)], axis=1))
    edge = edge[:8] + join(jnp.dot(arrived, edge_tab[...], preferred_element_type=F32))
    send_r[...] = edge
    send(10, 11)
    state = state[:8] + join(jnp.dot(arrived, slot_tab[...], preferred_element_type=F32))
    vel, mass = state[3:6], state[6:7]
    gathered = pick(state, ends[:grains, :])

    @pl.when(mine)
    def _():
        receive(22)
        for k in range(4):
            put_one_hot(
                cross_tab.at[k * half : (k + 1) * half, :],
                recv_e[8 + k : 9 + k, :].astype(jnp.int32), 1,
            )
        receive(20, 21, 19, 18, 26, 27, 25, 24)
        seen = split(jnp.concatenate([recv_x[k] for k in range(4)], axis=1))
        recv_r[top.astype(jnp.int32)] = recv_e[:8] + join(
            jnp.dot(seen, cross_tab[...], preferred_element_type=F32)
        )

    receive(10, 11)
    left, right = recv_r[0], recv_r[1]
    gathered += pick(jnp.concatenate([left, right], axis=1), ends[grains:extent, :])
    normal = gathered[0:3]
    speed = jnp.sum(normal * gathered[3:6], axis=0, keepdims=True)
    lam = jnp.maximum(0.0, lam - (pull + speed) / diag)
    force = rows8(normal * lam)
    partial = spread(force, ends[grains:, :])[0:3]
    ghost_left, ghost_right = partial[:, :width], partial[:, width : 2 * width]
    at_rim = partial[:, 2 * width :]
    send_c[0] = rows8(ghost_right, at_rim)
    send_c[1] = rows8(ghost_left, at_rim)
    send(12, 13, 14, 15)
    local = spread(force, ends[:grains, :])[0:3]
    base = pick(rows8(vel + mass * local), ends[:grains, :])[0:3]
    pull = coupled(lam)

    receive(12, 13, 14, 15)
    incoming = edge[6:7] * (recv_c[0, 0:3] + recv_c[1, 0:3])
    fresh_left = left[3:6] + left[6:7] * (recv_c[0, 3:6] + ghost_left + recv_c[2, 0:3])
    fresh_right = right[3:6] + right[6:7] * (recv_c[1, 3:6] + ghost_right + recv_c[3, 0:3])
    relative = base + pick(
        rows8(jnp.concatenate([fresh_left, fresh_right, incoming], axis=1)), ends[grains:, :]
    )[0:3]
    speed = jnp.sum(normal * relative, axis=0, keepdims=True)
    lam = jnp.maximum(0.0, lam - (pull + speed) / diag)
    force = rows8(normal * lam)
    partial = spread(force, ends[grains:extent, :])
    send_f[0] = partial[:, width:]
    send_f[1] = partial[:, :width]
    send(16, 17)
    lam_out[...] = lam
    base = vel + mass * spread(force, ends[:grains, :])[0:3]
    settled(*range(16), *range(18, MESSAGES))

    receive(16, 17)
    vel_out[...] = base + mass * spread(recv_f[0] + recv_f[1], rim_tab[...])[0:3]
    settled(16, 17)


def settle(vel_ref, lam_ref, vel_out, lam_out, sem):
    moves = [
        pltpu.make_async_copy(vel_ref, vel_out, sem.at[0]),
        pltpu.make_async_copy(lam_ref, lam_out, sem.at[1]),
    ]
    for move in moves:
        move.start()
    for move in moves:
        move.wait()


def body(count, positions, velocity, inv_mass, swap_lists, rim_list, contact_pair, delassus):
    grains = positions.shape[1]
    half = swap_lists.shape[1]
    width = rim_list.shape[0]
    contacts = contact_pair.shape[1]
    tiles, tile = delassus.shape[:2]
    args = (
        positions, velocity, inv_mass.reshape(1, grains), swap_lists, rim_list.reshape(1, width),
        contact_pair, delassus,
    )
    args = tuple(pltpu.with_memory_space_constraint(arg, pltpu.HBM) for arg in args)

    current, lam = pl.pallas_call(
        lambda *refs: kernel(count, *refs),
        out_shape=(
            jax.ShapeDtypeStruct((3, grains), F32),
            jax.ShapeDtypeStruct((1, contacts), F32),
        ),
        in_specs=[pl.BlockSpec(memory_space=pltpu.HBM)] * len(args),
        out_specs=(
            pl.BlockSpec(memory_space=pltpu.VMEM),
            pl.BlockSpec(memory_space=pltpu.VMEM),
        ),
        scratch_shapes=[pltpu.VMEM(arg.shape, arg.dtype) for arg in args]
        + [
            pltpu.VMEM((grains + 3 * width, contacts), BF16),
            pltpu.VMEM((4, grains, half), BF16),
            pltpu.VMEM((4, grains, half), BF16),
            pltpu.VMEM((2, grains, half), BF16),
            pltpu.VMEM((grains, width), BF16),
            pltpu.VMEM((4 * half, grains), BF16),
            pltpu.VMEM((4 * half, width), BF16),
            pltpu.VMEM((4 * half, width), BF16),
            pltpu.VMEM((contacts, tile), BF16),
            pltpu.VMEM((contacts, tile), BF16),
            pltpu.VMEM((8, half), F32),
            pltpu.VMEM((8, grains), F32),
            pltpu.VMEM((8, width), F32),
            pltpu.VMEM((2, 8, width), F32),
            pltpu.VMEM((2, 8, width), F32),
            pltpu.VMEM((16, width), F32),
            pltpu.VMEM((4, 8, half), F32),
            pltpu.VMEM((3, 3, half), jnp.int32),
            pltpu.VMEM((3, 8, grains), F32),
            pltpu.VMEM((2, 8, width), F32),
            pltpu.VMEM((4, 8, width), F32),
            pltpu.VMEM((2, 8, width), F32),
            pltpu.VMEM((4, 8, half), F32),
            pltpu.VMEM((16, width), F32),
            pltpu.VMEM((8, half), F32),
            pltpu.SemaphoreType.DMA((len(args),)),
            pltpu.SemaphoreType.DMA((MESSAGES,)),
            pltpu.SemaphoreType.DMA((MESSAGES,)),
            pltpu.SemaphoreType.REGULAR((4,)),
            pltpu.SemaphoreType.REGULAR((4,)),
            pltpu.SemaphoreType.REGULAR((4,)),
            pltpu.SemaphoreType.REGULAR,
            pltpu.SemaphoreType.REGULAR,
        ],
        compiler_params=pltpu.CompilerParams(
            collective_id=0, has_side_effects=True, vmem_limit_bytes=32 << 20
        ),
        name="contact_step",
    )(*args)
    current, lam = pl.pallas_call(
        settle,
        out_shape=(
            jax.ShapeDtypeStruct((3, grains), F32),
            jax.ShapeDtypeStruct((1, contacts), F32),
        ),
        in_specs=[pl.BlockSpec(memory_space=pl.ANY)] * 2,
        out_specs=(
            pl.BlockSpec(memory_space=pltpu.HBM), pl.BlockSpec(memory_space=pltpu.HBM)
        ),
        scratch_shapes=[pltpu.SemaphoreType.DMA((2,))],
        name="settle",
    )(
        pltpu.with_memory_space_constraint(current, pltpu.VMEM),
        pltpu.with_memory_space_constraint(lam, pltpu.VMEM),
    )
    return current, lam.reshape(contacts)


def solution(mesh):
    count = mesh.shape["parts"]
    in_specs = (
        P(None, "parts"),
        P(None, "parts"),
        P("parts"),
        P(None, "parts"),
        P("parts"),
        P(None, "parts"),
        P("parts", None, None),
    )
    out_specs = (P(None, "parts"), P("parts"))
    return jax.shard_map(
        lambda *args: body(count, *args),
        mesh=mesh, in_specs=in_specs, out_specs=out_specs, check_vma=False,
    )
```
